32 devices in a mesh: dp: 4 (over x, core), fsdp: 8 (over z, y).
Axes of the slice: x: 2, y: 2, z: 4, core: 2. Of those that a mesh axis runs over, the one named last changes fastest.
Arguments:
- tokens: bfloat16 [8192, 1024], P(('dp', 'fsdp')), may hold values from -6 to 6
- patch_counts: int32 [32, 4], P(('dp', 'fsdp')), may hold values from 0 to 256, as said below
- norm_one_gain: bfloat16 [1024], P('fsdp'), may hold values from 0.25 to 1.75
- norm_one_shift: bfloat16 [1024], P('fsdp'), may hold values from -3 to 3
- joint_weight: bfloat16 [1024, 3072], P('fsdp'), may hold values from -0.1875 to 0.1875
- query_bias: bfloat16 [1024], P('fsdp'), may hold values from -3 to 3
- value_bias: bfloat16 [1024], P('fsdp'), may hold values from -3 to 3
- output_weight: bfloat16 [1024, 1024], P('fsdp'), may hold values from -1 to 1
- output_bias: bfloat16 [1024], P('fsdp'), may hold values from -3 to 3
- norm_two_gain: bfloat16 [1024], P('fsdp'), may hold values from 0.25 to 1.75
- norm_two_shift: bfloat16 [1024], P('fsdp'), may hold values from -3 to 3
- expand_weight: bfloat16 [1024, 4096], P('fsdp'), may hold values from -0.1875 to 0.1875
- expand_bias: bfloat16 [4096], P('fsdp'), may hold values from -3 to 3
- shrink_weight: bfloat16 [4096, 1024], P('fsdp'), may hold values from -0.09375 to 0.09375
- shrink_bias: bfloat16 [1024], P('fsdp'), may hold values from -3 to 3
- cotangent: bfloat16 [8192, 1024], P(('dp', 'fsdp')), may hold values from -6 to 6
Outputs:
- output: bfloat16 [8192, 1024], P(('dp', 'fsdp'))
- tokens_grad: bfloat16 [8192, 1024], P(('dp', 'fsdp'))
- grad_norm_one_gain: float32 [1024], P('fsdp')
- grad_norm_one_shift: float32 [1024], P('fsdp')
- grad_joint_weight: float32 [1024, 3072], P('fsdp')
- grad_query_bias: float32 [1024], P('fsdp')
- grad_value_bias: float32 [1024], P('fsdp')
- grad_output_weight: float32 [1024, 1024], P('fsdp')
- grad_output_bias: float32 [1024], P('fsdp')
- grad_norm_two_gain: float32 [1024], P('fsdp')
- grad_norm_two_shift: float32 [1024], P('fsdp')
- grad_expand_weight: float32 [1024, 4096], P('fsdp')
- grad_expand_bias: float32 [4096], P('fsdp')
- grad_shrink_weight: float32 [4096, 1024], P('fsdp')
- grad_shrink_bias: float32 [1024], P('fsdp')
The draws below stay inside these ranges and needn't reach their ends.
Inputs may be any that keep to these rules, and one draw needn't show every extreme that they name: `patch_counts`: row d lists the patch counts of device d's images in its first slots, zeros after them. A device holds one image of 256 patches, or one or two of 128, or two to four of 64; each kind occurs on some device.
All inputs are finite; a program needn't handle non-finite values.
Results may differ from the reference program's by a relative error of at most 0.019.
Values may be sent and summed in bfloat16 or wider, within the bound.
A program may use at most 192 MiB of HBM per device.

```python
import jax
import jax.numpy as jnp
from jax import lax

D = 1024
FF = 4096
HEADS = 16
HEAD_DIM = 64
CAP = 256
IMG_DEV = 4
ROWS = 8192
N_DP = 4
N_FSDP = 8


def draw_patch_counts(key, part):
    device_count = ROWS // CAP
    key_order = jax.random.fold_in(key, 11)
    key_more = jax.random.fold_in(key, 12)
    order = jax.random.permutation(key_order, device_count)
    kinds = order % 3
    extra = jax.random.randint(key_more, (device_count,), 0, 3)
    images = jnp.where(kinds == 0, 1, jnp.where(kinds == 1, 1 + jnp.minimum(extra, 1), 2 + extra))
    length = jnp.where(kinds == 0, CAP, jnp.where(kinds == 1, CAP // 2, CAP // 4))
    slots = jnp.arange(IMG_DEV, dtype=jnp.int32)
    return jnp.where(slots[None, :] < images[:, None], length[:, None], 0).astype(jnp.int32)


def block_levels(rng, dims, shards, least, largest):
    level, own = 1.0, jax.random.fold_in(rng, 6)
    for position, blocks in shards:
        heights = jnp.exp(jax.random.uniform(jax.random.fold_in(own, position), (blocks,), jnp.float32, least / len(shards), largest / len(shards)))
        level = level * jnp.repeat(heights, dims[position] // blocks).reshape([-1 if axis == position else 1 for axis in range(len(dims))])
    return level


def bell_draw(key, extent, width, limit, split=(), held_as=jnp.bfloat16):
    array = width * jax.random.normal(key, extent, jnp.float32)
    if split:
        array = array * block_levels(key, extent, split, -0.22, 0.18)
    return jnp.clip(array, -limit, limit).astype(held_as)


def setup_inputs(seed: int = 0) -> dict:
    key_of = jax.random.split(jax.random.key(seed), 17)
    return {
        "tokens": bell_draw(key_of[0], (ROWS, D), 1.0, 6.0, ((0, 32),)),
        "patch_counts": draw_patch_counts(jax.random.fold_in(key_of[16], 71), 0),
        "norm_one_gain": jnp.clip(1.0 + 0.15 * jax.random.normal(key_of[2], (D,), jnp.float32), 0.25, 1.75).astype(jnp.bfloat16),
        "norm_one_shift": bell_draw(key_of[3], (D,), 0.5, 3.0, ((0, 8),)),
        "joint_weight": bell_draw(key_of[4], (D, 3 * D), D ** -0.5, 0.1875, ((0, 8),)),
        "query_bias": bell_draw(key_of[5], (D,), 0.5, 3.0, ((0, 8),)),
        "value_bias": bell_draw(key_of[6], (D,), 0.5, 3.0, ((0, 8),)),
        "output_weight": bell_draw(key_of[7], (D, D), (D // 32) ** -0.5, 1.0, ((0, 8),)),
        "output_bias": bell_draw(key_of[8], (D,), 0.5, 3.0, ((0, 8),)),
        "norm_two_gain": jnp.clip(1.0 + 0.15 * jax.random.normal(key_of[9], (D,), jnp.float32), 0.25, 1.75).astype(jnp.bfloat16),
        "norm_two_shift": bell_draw(key_of[10], (D,), 0.5, 3.0, ((0, 8),)),
        "expand_weight": bell_draw(key_of[11], (D, FF), D ** -0.5, 0.1875, ((0, 8),)),
        "expand_bias": bell_draw(key_of[12], (FF,), 0.5, 3.0, ((0, 8),)),
        "shrink_weight": bell_draw(key_of[13], (FF, D), FF ** -0.5, 0.09375, ((0, 8),)),
        "shrink_bias": bell_draw(key_of[14], (D,), 0.5, 3.0, ((0, 8),)),
        "cotangent": bell_draw(key_of[15], (ROWS, D), 1.0, 6.0, ((0, 32),)),
    }


@jax.custom_vjp
def low(v):
    return lax.optimization_barrier(v.astype(jnp.bfloat16)).astype(jnp.float32)

@jax.custom_vjp
def low_back(v):
    return v

def low_keep(v):
    return (low(v), None)

def low_pass(kept, grad):
    return (grad,)

def back_keep(v):
    return (v, None)

def back_low(kept, grad):
    return (low(grad),)
low.defvjp(low_keep, low_pass)
low_back.defvjp(back_keep, back_low)
epsilon = 1e-05
masked_score = -1e+30
highest = lax.Precision.HIGHEST

def product(left, right):
    return jnp.dot(left, right, precision=highest, preferred_element_type=jnp.float32)

def norm_rows(values, gain, shift):
    centre = lax.optimization_barrier(jnp.mean(values, axis=-1, keepdims=True))
    centred = values - centre
    spread = lax.optimization_barrier(jnp.mean(centred * centred, axis=-1, keepdims=True))
    return centred * lax.rsqrt(spread + epsilon) * gain + shift

def image_rows(counts):
    ends = jnp.cumsum(counts).astype(jnp.int32)
    places = jnp.arange(CAP, dtype=jnp.int32)
    images = lax.optimization_barrier(jnp.sum((places[:, None] >= ends[None, :]).astype(jnp.int32), axis=1))
    living = (places < ends[-1]).astype(jnp.float32)
    return (images, living)

def attend_image(bundle):
    queries, keys_all, values_all, images = bundle
    query_heads = queries.reshape(CAP, HEADS, HEAD_DIM)
    key_heads = keys_all.reshape(CAP, HEADS, HEAD_DIM)
    value_heads = values_all.reshape(CAP, HEADS, HEAD_DIM)
    raw = jnp.einsum('qhd,khd->hqk', query_heads, key_heads, precision=highest) * HEAD_DIM ** (-0.5)
    same = images[:, None] == images[None, :]
    scores = low_back(jnp.where(same[None, :, :], raw, masked_score))
    weights = jax.nn.softmax(scores, axis=-1)
    mixed = jnp.einsum('hqk,khd->qhd', low(weights), value_heads, precision=highest)
    return mixed.reshape(CAP, D)

def layer(params, inputs, images, living):
    gain_one, shift_one, joint_w, query_b, value_b, out_w, out_b, gain_two, shift_two, expand_w, expand_b, shrink_w, shrink_b = params
    flat = inputs.reshape(-1, D)
    normed_one = low(norm_rows(flat, gain_one, shift_one))
    joint = product(normed_one, joint_w)
    queries = low(low_back(joint[:, :D] + query_b))
    keys_all = low(low_back(joint[:, D:2 * D]))
    values_all = low(low_back(joint[:, 2 * D:] + value_b))
    blocks = (queries.reshape(-1, CAP, D), keys_all.reshape(-1, CAP, D), values_all.reshape(-1, CAP, D), images)
    mixed = lax.map(jax.checkpoint(attend_image), blocks)
    mixed = low(low_back(mixed.reshape(-1, D)))
    first = flat + low_back(product(mixed, out_w) + out_b)
    normed_two = low(norm_rows(first, gain_two, shift_two))
    hidden_pre = low_back(product(normed_two, expand_w) + expand_b)
    hidden_act = low(jax.nn.gelu(hidden_pre, approximate=False))
    result = first + low_back(product(hidden_act, shrink_w) + shrink_b)
    return result * living.reshape(-1, 1)

def reference(tokens, patch_counts, norm_one_gain, norm_one_shift, joint_weight, query_bias, value_bias, output_weight, output_bias, norm_two_gain, norm_two_shift, expand_weight, expand_bias, shrink_weight, shrink_bias, cotangent):
    params = tuple((p.astype(jnp.float32) for p in (norm_one_gain, norm_one_shift, joint_weight, query_bias, value_bias, output_weight, output_bias, norm_two_gain, norm_two_shift, expand_weight, expand_bias, shrink_weight, shrink_bias)))
    device_count = N_DP * N_FSDP
    group = max(1, min(device_count, 4096 // CAP))
    rounds = device_count // group
    inputs_all = tokens.reshape(rounds, group, CAP, D)
    cot_all = cotangent.reshape(rounds, group * CAP, D)
    counts_all = patch_counts.reshape(rounds, group, IMG_DEV)

    def one_round(totals, item):
        inputs, cot, counts = item
        images, living = jax.vmap(image_rows)(counts)

        def forward(prm, values):
            return layer(prm, values, images, living)
        result, pull = jax.vjp(forward, params, inputs.astype(jnp.float32))
        prm_grad, input_grad = pull(cot.astype(jnp.float32))
        totals = jax.tree.map(lambda whole, part: whole + part, totals, prm_grad)
        return (totals, (result.astype(jnp.bfloat16), input_grad.reshape(-1, D).astype(jnp.bfloat16)))
    zeros = tuple((jnp.zeros_like(p) for p in params))
    totals, (results, input_grads) = lax.scan(one_round, zeros, (inputs_all, cot_all, counts_all))
    grads = tuple((t / float(device_count) for t in totals))
    return (results.reshape(ROWS, D), input_grads.reshape(ROWS, D), grads[0], grads[1], grads[2], grads[3], grads[4], grads[5], grads[6], grads[7], grads[8], grads[9], grads[10], grads[11], grads[12])
```

```python
import functools
from types import SimpleNamespace

import jax
import jax.numpy as jnp
from jax import lax
from jax.experimental import pallas as pl
from jax.experimental.pallas import tpu as pltpu
from jax.sharding import PartitionSpec as P

HEADS = 16
EPS = 1e-05
MASKED = -1e30
MESH = pl.DeviceIdType.MESH
BF = jnp.bfloat16
F32 = jnp.float32
VROWS = 16
J, O, E, S, VEC = range(5)


class Sizes:
    def __init__(self, n_dp, n_fsdp, rows, width, hidden, slots):
        self.n_dp, self.n = n_dp, n_fsdp
        self.R, self.D, self.FF, self.slots = rows, width, hidden, slots
        self.Y = 2 ** ((n_fsdp.bit_length() - 1) // 2)
        self.Z = n_fsdp // self.Y
        T = 4 if n_dp % 4 == 0 else 2
        while hidden // n_fsdp // T % 128 or self.Z % T:
            T //= 2
        self.T, self.X = T, T // 2
        self.RT = T * rows
        self.Dn = width // n_fsdp
        self.DT = width // T
        self.H = HEADS // T
        self.hd = width // HEADS
        self.F = hidden // T
        self.FB = hidden // n_fsdp // T
        self.ZT = self.Z // T


def dot_nn(a, b):
    return jnp.dot(a, b, preferred_element_type=F32)


def dot_nt(a, b):
    return lax.dot_general(a, b, (((1,), (1,)), ((), ())), preferred_element_type=F32)


def dot_tn(a, b):
    return lax.dot_general(a, b, (((0,), (0,)), ((), ())), preferred_element_type=F32)


def ds(start, size, mult):
    return pl.ds(pl.multiple_of(start, mult), size)


def norm_parts(x):
    mean = jnp.mean(x, axis=-1, keepdims=True)
    xc = x - mean
    var = jnp.mean(xc * xc, axis=-1, keepdims=True)
    s = lax.rsqrt(var + EPS)
    return xc * s, s


def layout(q):
    R, D, T, RT = q.R, q.D, q.T, q.RT
    Cj = 3 * q.DT
    DMA = pltpu.SemaphoreType.DMA
    V = pltpu.VMEM
    m = SimpleNamespace()
    m.tok = V((T, R, D), BF)
    m.n1 = V((RT, D), BF)
    m.cot = V((T, R, D), BF)
    m.w = [V((D, Cj), BF), V((q.DT, D), BF), V((D, q.F), BF), V((q.F, D), BF)]
    m.qkv = V((RT, Cj), BF)
    m.prob = V((T * q.H, R, R), BF)
    m.mixed = V((RT, q.DT), BF)
    m.first = V((R, D), F32)
    m.n2 = V((T, R, D), BF)
    m.hact = V((RT, q.F), BF)
    m.dgelu = V((RT, q.F), BF)
    m.hgrad = V((RT, q.F), BF)
    m.proj = V((T, R, D), BF)
    m.fgrad = V((R, D), F32)
    m.mgrad = V((RT, q.DT), BF)
    m.jgrad = V((RT, Cj), BF)
    m.obuf = V((R, D), BF)
    m.tbuf = V((R, D), BF)
    m.acc0 = V((R, D), F32)
    m.psend = [V((q.X, R, D), BF) for _ in range(2)]
    m.precv = [V((q.X, R, D), BF) for _ in range(2)]
    m.xsend = [V((R, D) if q.X == 2 else (16, 128), BF) for _ in range(2)]
    m.xrecv = [V((R, D) if q.X == 2 else (16, 128), BF) for _ in range(2)]
    m.rs = [[DMA((q.X,)), DMA((q.X,)), DMA((1,)), DMA((1,))] for _ in range(4)]
    m.dw = [V((bz, q.Y * rb, C), BF) for bz, rb, C in q.grads]
    m.yr = [V((q.Y - 1, bz, rb, C), BF) for bz, rb, C in q.grads]
    m.zr = [V((q.Z - 1, rb, C), BF) for bz, rb, C in q.grads]
    m.fin = [V((1 if w == O else T, rb, C), BF) for w, (bz, rb, C) in enumerate(q.grads)]
    m.sy = [[DMA((q.Y - 1, bz)), DMA((q.Y - 1, bz))] for bz, rb, C in q.grads]
    m.sz = [[DMA((q.Z - 1,)), DMA((q.Z - 1,))] for _ in q.grads]
    m.sout = [DMA((T, q.n)) for _ in q.grads]
    m.gz = [[DMA((q.Z - 1,)), DMA((max(q.Z - 1, q.ZT),))] for _ in range(5)]
    m.gy = [[DMA((q.Y - 1, q.Z)), DMA((q.Y - 1, q.Z))] for _ in range(5)]
    pair = lambda: [DMA((3,)), DMA((3,))]
    m.ttok, m.tcot, m.tn2, m.tproj, m.tcnt, m.tfo = (pair() for _ in range(6))
    m.tfin = [pair() for _ in q.grads]
    m.vec = V((q.n, VROWS, q.Dn), BF)
    m.vf = V((8, D), F32)
    m.hb = V((8, q.F), F32)
    m.cnt = V((T, 8, 128), jnp.int32)
    m.vg = V((8, D), F32)
    m.vgh = V((8, q.F), F32)
    m.v3 = V((q.n, VROWS, q.Dn), F32)
    m.v3c = V((2, q.n, VROWS, q.Dn), F32)
    m.v3y = V((q.Y - 1, q.Z, VROWS, q.Dn), F32)
    m.v3s = V((q.Z, VROWS, q.Dn), F32)
    m.v3z = V((q.Z - 1, VROWS, q.Dn), F32)
    m.vout = V((VROWS, q.Dn), F32)
    m.svt = [DMA((2,)), DMA((2,))]
    m.svy = [DMA((q.Y - 1, q.Z)), DMA((q.Y - 1, q.Z))]
    m.svz = [DMA((q.Z - 1,)), DMA((q.Z - 1,))]
    m.loc = DMA((7 + q.n,))
    return vars(m)


def kernel(q, tree, *refs):
    (tokens, counts, joint_w, out_w, exp_w, shr_w, cotangent) = refs[:7]
    vectors = refs[7:16]
    (o_out, o_tg, o_vec, o_j, o_o, o_e, o_s) = refs[16:23]
    b = SimpleNamespace(**jax.tree.unflatten(tree, refs[23:]))
    R, D, T, X, RT, n, Y, Z = q.R, q.D, q.T, q.X, q.RT, q.n, q.Y, q.Z
    Dn, DT, F, FB, H, hd, ZT = q.Dn, q.DT, q.F, q.FB, q.H, q.hd, q.ZT
    Cj = 3 * DT

    dp = lax.axis_index("dp")
    s = lax.axis_index("fsdp")
    t = dp % T
    c, xx = t % 2, t // 2
    y, z = s % Y, s // Y
    core = (dp + 1 - 2 * c, s)
    xdp = dp + 2 - 4 * xx
    xpeer = (xdp, s)
    xcore = (xdp + 1 - 2 * c, s)
    tc = t + 1 - 2 * c
    if X == 2:
        tx = t + 2 - 4 * xx
        txc = tx + 1 - 2 * c
    zid = [(z + k) % Z for k in range(Z)]
    zsrc = [(z + Z - k) % Z for k in range(Z)]
    yid = [(y + k) % Y for k in range(Y)]
    ysrc = [(y + Y - k) % Y for k in range(Y)]
    zpeer = [(dp, zid[k] * Y + y) for k in range(Z)]
    ypeer = [(dp, z * Y + yid[k]) for k in range(Y)]
    pending = []

    def rc(src, dst, ss, rs, dev):
        return pltpu.make_async_remote_copy(
            src_ref=src, dst_ref=dst, send_sem=ss, recv_sem=rs,
            device_id=dev, device_id_type=MESH)

    def go(cp):
        cp.start()
        pending.append(cp)
        return cp

    loc = b.loc
    cp_tok = pltpu.make_async_copy(tokens, b.tok.at[t], loc.at[0])
    cp_cot = pltpu.make_async_copy(cotangent, b.cot.at[t], loc.at[1])
    cp_shr = pltpu.make_async_copy(
        shr_w.at[ds(t * FB, FB, 16)], b.w[S].at[ds(s * FB, FB, 16)], loc.at[3])
    cp_j = [pltpu.make_async_copy(
        joint_w.at[:, ds(j * D + t * DT, DT, 128)],
        b.w[J].at[ds(s * Dn, Dn, 16), pl.ds(j * DT, DT)], loc.at[4 + j]) for j in range(3)]
    cp_e = [pltpu.make_async_copy(
        exp_w.at[:, ds(i * (T * FB) + t * FB, FB, 128)],
        b.w[E].at[ds(s * Dn, Dn, 16), pl.ds(i * FB, FB)], loc.at[7 + i]) for i in range(n)]
    for cp in cp_j + [cp_tok] + cp_e + [cp_shr, cp_cot]:
        cp.start()

    lane = lax.broadcasted_iota(jnp.int32, (8, 128), 1)
    cv = jnp.zeros((8, 128), jnp.int32)
    for i in range(q.slots):
        cv = jnp.where(lane == i, counts[0, i], cv)
    b.cnt[t] = cv

    bar = pltpu.get_barrier_semaphore()
    greet = [core] + ([xpeer, xcore] if X == 2 else []) + zpeer[1:] + ypeer[1:]
    for dev in greet:
        pl.semaphore_signal(bar, inc=1, device_id=dev, device_id_type=MESH)
    pl.semaphore_wait(bar, len(greet))

    def slot(w, src_s):
        if w == VEC:
            return b.vec.at[src_s]
        if w == S:
            return b.w[S].at[ds(src_s * FB, FB, 16)]
        return b.w[w].at[ds(src_s * Dn, Dn, 16)]

    def ag_z(w):
        for k in range(1, Z):
            go(rc(slot(w, s), slot(w, s), b.gz[w][0].at[k - 1], b.gz[w][1].at[k - 1], zpeer[k]))

    def ag_y(w, k):
        src = zsrc[k] * Y + y
        if k:
            rc(slot(w, src), slot(w, src), b.gz[w][0].at[k - 1], b.gz[w][1].at[k - 1], zpeer[k]).wait_recv()
        for m in range(1, Y):
            go(rc(slot(w, src), slot(w, src), b.gy[w][0].at[m - 1, k], b.gy[w][1].at[m - 1, k], ypeer[m]))

    def ag_wait(w):
        for k in range(Z):
            for m in range(1, Y):
                src = zsrc[k] * Y + ysrc[m]
                rc(slot(w, src), slot(w, src), b.gy[w][0].at[m - 1, k], b.gy[w][1].at[m - 1, k], ypeer[m]).wait_recv()

    zlo = t * ZT
    mine = z // ZT == t

    def wo_slot(zz, yy):
        return b.w[O].at[ds((zz * Y + yy) * Dn, Dn, 16)]

    def wo_z():
        @pl.when(mine)
        def _():
            zz = z - zlo
            for k in range(1, Z):
                rc(out_w, wo_slot(zz, y), b.gz[O][0].at[k - 1], b.gz[O][1].at[zz], zpeer[k]).start()
            pltpu.make_async_copy(out_w, wo_slot(zz, y), b.gz[O][1].at[zz]).start()

    def wo_y():
        for zz in range(ZT):
            pltpu.make_async_copy(out_w, wo_slot(zz, y), b.gz[O][1].at[zz]).wait()
            for m in range(1, Y):
                go(rc(wo_slot(zz, y), wo_slot(zz, y), b.gy[O][0].at[m - 1, zz], b.gy[O][1].at[m - 1, zz], ypeer[m]))

    def wo_wait():
        for zz in range(ZT):
            for m in range(1, Y):
                rc(wo_slot(zz, ysrc[m]), wo_slot(zz, ysrc[m]), b.gy[O][0].at[m - 1, zz], b.gy[O][1].at[m - 1, zz], ypeer[m]).wait_recv()

    def wo_drain():
        @pl.when(mine)
        def _():
            for k in range(1, Z):
                rc(out_w, wo_slot(z - zlo, y), b.gz[O][0].at[k - 1], b.gz[O][1].at[0], zpeer[k]).wait_send()

    def tp_send(buf, w, src=None):
        src = buf.at[t] if src is None else src
        if X == 2:
            go(rc(src, buf.at[t], w[0].at[1], w[1].at[1], xpeer))
        go(rc(src, buf.at[t], w[0].at[0], w[1].at[0], core))

    def tp_core(buf, w):
        rc(buf.at[tc], buf.at[tc], w[0].at[0], w[1].at[0], core).wait_recv()

    def tp_x(buf, w):
        if X == 2:
            rc(buf.at[tx], buf.at[tx], w[0].at[1], w[1].at[1], xpeer).wait_recv()
            go(rc(buf.at[tx], buf.at[tx], w[0].at[2], w[1].at[2], core))

    def tp_last(buf, w):
        if X == 2:
            rc(buf.at[txc], buf.at[txc], w[0].at[2], w[1].at[2], core).wait_recv()

    order = [(t, None), (tc, tp_core)] + ([(tx, tp_x), (txc, tp_last)] if X == 2 else [])

    vrow = lax.broadcasted_iota(jnp.int32, (VROWS, Dn), 0)
    packed = jnp.zeros((VROWS, Dn), F32)
    pieces = [v[...] for v in vectors[:8]]
    pieces += [vectors[8][pl.ds(r * Dn, Dn)] for r in range(vectors[8].shape[0] // Dn)]
    for i, piece in enumerate(pieces):
        packed = jnp.where(vrow == i, piece.astype(F32).reshape(1, Dn), packed)
    b.vec[s] = packed.astype(BF)
    ag_z(VEC)
    ag_y(VEC, 0)
    cnt = b.cnt
    peers = [core] + ([xpeer, xcore] if X == 2 else [])
    for i, dev in enumerate(peers):
        go(rc(cnt.at[t], cnt.at[t], b.tcnt[0].at[i], b.tcnt[1].at[i], dev))
    for cp in cp_j:
        cp.wait()
    ag_z(J)
    ag_y(J, 0)
    cp_tok.wait()
    tp_send(b.tok, b.ttok)
    wo_z()
    for cp in cp_e:
        cp.wait()
    ag_z(E)
    cp_shr.wait()
    ag_z(S)

    for k in range(1, Z):
        ag_y(VEC, k)
    ag_wait(VEC)
    vf, hb = b.vf, b.hb
    for i in range(n):
        piece = b.vec[i].astype(F32)
        vf[:, i * Dn:(i + 1) * Dn] = piece[0:8]
        kk = FB // Dn
        for r in range(kk):
            row = piece[8 + r:9 + r]
            for g in range(1, T):
                row = jnp.where(t == g, piece[8 + g * kk + r:9 + g * kk + r], row)
            hb[0:1, i * FB + r * Dn:i * FB + (r + 1) * Dn] = row
    vg, vgh = b.vg, b.vgh
    vg[...] = jnp.zeros_like(vg)

    for i, st in enumerate([tc] + ([tx, txc] if X == 2 else [])):
        rc(cnt.at[st], cnt.at[st], b.tcnt[0].at[i], b.tcnt[1].at[i], peers[i]).wait_recv()

    def ends_of(g):
        row = cnt[g]
        ends, total = [], None
        for i in range(q.slots):
            v = row[0:1, i:i + 1]
            total = v if total is None else total + v
            ends.append(total)
        return ends

    RB = 64
    nrb = R // RB

    def live_of(ends, r0, rows):
        places = lax.broadcasted_iota(jnp.int32, (rows, 1), 0) + r0
        return (places < ends[-1]).astype(F32)

    own_ends = ends_of(t)
    cp_cot.wait()
    cot = b.cot

    def cot_step(i, acc):
        r0 = pl.multiple_of(i * RB, RB)
        v = cot[t, pl.ds(r0, RB), :].astype(F32) * live_of(own_ends, r0, RB)
        cot[t, pl.ds(r0, RB), :] = v.astype(BF)
        return acc + jnp.sum(v, axis=0, keepdims=True)

    vg[7:8, :] = lax.fori_loop(0, nrb, cot_step, jnp.zeros((1, D), F32))
    tp_send(cot, b.tcot)

    tok, n1 = b.tok, b.n1

    def ln1(g):
        def step(i, _):
            r0 = pl.multiple_of(i * RB, RB)
            nn, _s = norm_parts(tok[g, pl.ds(r0, RB), :].astype(F32))
            n1[ds(g * R + r0, RB, RB), :] = (nn * vf[0:1, :] + vf[1:2, :]).astype(BF)
            return 0
        lax.fori_loop(0, nrb, step, 0)

    for g, arrive in order:
        if arrive is not None:
            arrive(tok, b.ttok)
        ln1(g)

    for k in range(1, Z):
        ag_y(J, k)
    wo_y()
    ag_y(E, 0)
    tp_core(cot, b.tcot)
    tp_x(cot, b.tcot)
    ag_wait(J)

    qkv, wj = b.qkv, b.w[J]
    TN = 256
    for j in range(3):
        def step(i, _, j=j):
            col = j * DT + i * TN
            r = dot_nn(n1[...], wj[:, ds(col, TN, 128)])
            if j != 1:
                r = r + vf[(2 if j == 0 else 3):(3 if j == 0 else 4), ds(t * DT + i * TN, TN, 128)]
            qkv[:, ds(col, TN, 128)] = r.astype(BF)
            return 0
        lax.fori_loop(0, DT // TN, step, 0)

    scale = hd ** (-0.5)
    prob, mixed = b.prob, b.mixed
    AW = 256
    GH = AW // hd
    lanes = lax.broadcasted_iota(jnp.int32, (1, AW), 1)
    head_masks = [(lanes // hd == h) for h in range(GH)]

    def hm(v, h):
        return jnp.where(head_masks[h], v, jnp.zeros_like(v))

    def attend(g):
        ends = ends_of(g)
        ri = lax.broadcasted_iota(jnp.int32, (R, R), 0)
        ci = lax.broadcasted_iota(jnp.int32, (R, R), 1)
        im_r = jnp.zeros((R, R), jnp.int32)
        im_c = jnp.zeros((R, R), jnp.int32)
        for e in ends:
            im_r = im_r + (ri >= e).astype(jnp.int32)
            im_c = im_c + (ci >= e).astype(jnp.int32)
        same = im_r == im_c
        rows = ds(g * R, R, 256)
        for a in range(DT // AW):
            qa = qkv[rows, pl.ds(a * AW, AW)]
            ka = qkv[rows, pl.ds(DT + a * AW, AW)]
            va = qkv[rows, pl.ds(2 * DT + a * AW, AW)]
            acc = None
            for h in range(GH):
                sc = dot_nt(hm(qa, h), ka) * scale
                sc = jnp.where(same, sc, MASKED)
                top = jnp.max(sc, axis=-1, keepdims=True)
                ex = jnp.exp(sc - top)
                tot = jnp.sum(ex, axis=-1, keepdims=True)
                p = (ex * (1.0 / tot)).astype(BF)
                prob[g * H + a * GH + h] = p
                part = dot_nn(p, hm(va, h))
                acc = part if acc is None else acc + part
            mixed[rows, pl.ds(a * AW, AW)] = acc.astype(BF)

    def att_step(g, _):
        attend(g)
        return 0

    lax.fori_loop(0, T // 2, att_step, 0)
    ag_y(E, 1)
    lax.fori_loop(T // 2, T, att_step, 0)
    wo_wait()

    acc0 = b.acc0

    def block_mm(lhs, g, rhs, nt, put):
        def step(i, _):
            cols = ds(i * TN, TN, 256)
            a = lhs[ds(g * R, R, 256), :]
            put(cols, dot_nt(a, rhs[cols, :]) if nt else dot_nn(a, rhs[:, cols]))
            return 0
        lax.fori_loop(0, D // TN, step, 0)

    def rs_copy(u, r, i):
        return rc(b.psend[u].at[i], b.precv[u].at[i], b.rs[r][0].at[i], b.rs[r][1].at[i], core)

    def rs_xcopy(u, r):
        return rc(b.xsend[u], b.xrecv[u], b.rs[r][2].at[0], b.rs[r][3].at[0], xpeer)

    def rs_start(u, r, lhs, rhs, nt):
        ps = b.psend[u]

        def put_at(i):
            def put(cols, v):
                ps[i, :, cols] = v.astype(BF)
            return put

        def put_acc(cols, v):
            acc0[:, cols] = v

        if X == 2:
            block_mm(lhs, txc, rhs, nt, put_at(1))
            rs_copy(u, r, 1).start()
            block_mm(lhs, tx, rhs, nt, put_acc)
            rs_copy(u, r, 1).wait_recv()
            pr, xs = b.precv[u], b.xsend[u]

            def add(i, _):
                rows = ds(i * RB, RB, RB)
                xs[rows, :] = (acc0[rows, :] + pr[1, rows, :].astype(F32)).astype(BF)
                return 0
            lax.fori_loop(0, nrb, add, 0)
            rs_xcopy(u, r).start()
        block_mm(lhs, tc, rhs, nt, put_at(0))
        rs_copy(u, r, 0).start()
        block_mm(lhs, t, rhs, nt, put_acc)

    def rs_wait(u, r):
        rs_copy(u, r, 0).wait_recv()
        if X == 2:
            rs_xcopy(u, r).wait_recv()

    def rs_value(u, rows):
        v = acc0[rows, :] + b.precv[u][0, rows, :].astype(F32)
        if X == 2:
            v = v + b.xrecv[u][rows, :].astype(F32)
        return v

    def rs_done(u, r):
        for i in range(X):
            rs_copy(u, r, i).wait_send()
        if X == 2:
            rs_xcopy(u, r).wait_send()

    rs_start(0, 0, mixed, b.w[O], False)
    tp_last(cot, b.tcot)
    for k in range(2, Z):
        ag_y(E, k)
    ag_y(S, 0)
    rs_wait(0, 0)
    first, n2 = b.first, b.n2

    def ln2(i, _):
        rows = ds(i * RB, RB, RB)
        v = tok[t, rows, :].astype(F32) + (rs_value(0, rows) + vf[4:5, :])
        first[rows, :] = v
        nn, _s = norm_parts(v)
        n2[t, rows, :] = (nn * vf[5:6, :] + vf[6:7, :]).astype(BF)
        return 0
    lax.fori_loop(0, nrb, ln2, 0)
    tp_send(n2, b.tn2)
    rs_done(0, 0)
    for k in range(1, Z):
        ag_y(S, k)
    ag_wait(E)

    hact, dgelu, we, ws = b.hact, b.dgelu, b.w[E], b.w[S]

    def up(g):
        def step(i, _):
            cols = ds(i * TN, TN, 256)
            rows = ds(g * R, R, 256)
            h = dot_nn(n2[g], we[:, cols]) + hb[0:1, cols]
            phi = 0.5 * (1.0 + lax.erf(h * 0.7071067811865476))
            hact[rows, cols] = (h * phi).astype(BF)
            dgelu[rows, cols] = (phi + h * (jnp.exp(-0.5 * h * h) * 0.3989422804014327)).astype(BF)
            return 0
        lax.fori_loop(0, F // TN, step, 0)

    for g, arrive in order:
        if arrive is not None:
            arrive(n2, b.tn2)
        up(g)

    def blocks(w):
        return q.grads[w]

    def dw_dest(w, k):
        return zlo + k if w == O else zid[k]

    def dw_slot(w, k):
        return k if w == O else zid[k]

    def dw_y(w, sl, m):
        rb = blocks(w)[1]
        return rc(b.dw[w].at[sl, ds(yid[m] * rb, rb, 16)], b.yr[w].at[m - 1, sl],
                  b.sy[w][0].at[m - 1, sl], b.sy[w][1].at[m - 1, sl], ypeer[m])

    def dw_compute(w, k, lhs, rhs):
        bz, rb, C = blocks(w)
        sl = dw_slot(w, k)
        tile = Y * rb
        TC = 256

        def step(i, _):
            cols = ds(i * TC, TC, 256)
            for r in range(tile // 256):
                a = lhs(sl * tile + r * 256)
                b.dw[w][sl, pl.ds(r * 256, 256), cols] = dot_tn(a, rhs(cols)).astype(BF)
            return 0
        lax.fori_loop(0, C // TC, step, 0)
        for m in range(1, Y):
            go(dw_y(w, sl, m))

    def dw_sum(w, k):
        bz, rb, C = blocks(w)
        sl = dw_slot(w, k)
        for m in range(1, Y):
            dw_y(w, sl, m).wait_recv()
        ch = 64

        def add(i, _):
            rows = ds(y * rb + i * ch, ch, 64)
            v = b.dw[w][sl, rows, :].astype(F32)
            for m in range(1, Y):
                v = v + b.yr[w][m - 1, sl, ds(i * ch, ch, 64), :].astype(F32)
            b.dw[w][sl, rows, :] = v.astype(BF)
            return 0
        lax.fori_loop(0, rb // ch, add, 0)

    def dw_z(w, k):
        rb = blocks(w)[1]
        return rc(b.dw[w].at[zid[k], ds(y * rb, rb, 16)], b.zr[w].at[k - 1],
                  b.sz[w][0].at[k - 1], b.sz[w][1].at[k - 1], zpeer[k])

    def dw_o(zz, k):
        return rc(b.dw[O].at[zz, ds(y * Dn, Dn, 16)], b.zr[O].at[k - 1],
                  b.sz[O][0].at[k - 1], b.sz[O][1].at[k - 1], zpeer[k])

    def dw_send(w, k):
        dw_sum(w, k)
        if k:
            go(dw_z(w, k))

    def dwo_send(drain=False):
        for zz in range(ZT):
            if not drain:
                dw_sum(O, zz)
            for k in range(1, Z):
                @pl.when(zid[k] == zlo + zz)
                def _(zz=zz, k=k):
                    if drain:
                        dw_o(zz, k).wait_send()
                    else:
                        dw_o(zz, k).start()

    def dw_final(w):
        bz, rb, C = blocks(w)
        for k in range(1, Z):
            (dw_o(0, k) if w == O else dw_z(w, k)).wait_recv()
        ch = 64
        fin = b.fin[w]
        own = z - zlo if w == O else z
        me = 0 if w == O else t

        def add(i, _):
            rows = ds(i * ch, ch, 64)
            v = b.dw[w][own, ds(y * rb + i * ch, ch, 64), :].astype(F32)
            for k in range(1, Z):
                v = v + b.zr[w][k - 1, rows, :].astype(F32)
            fin[me, rows, :] = v.astype(BF)
            return 0
        lax.fori_loop(0, rb // ch, add, 0)
        if w != O:
            tp_send(fin, b.tfin[w])

    def out_copies(w, g):
        fin, so = b.fin[w], b.sout[w]
        if w == J:
            return [pltpu.make_async_copy(fin.at[g, :, pl.ds(j * DT, DT)],
                    o_j.at[:, ds(j * D + g * DT, DT, 128)], so.at[g, j]) for j in range(3)]
        if w == E:
            return [pltpu.make_async_copy(fin.at[g, :, pl.ds(i * FB, FB)],
                    o_e.at[:, ds(i * (T * FB) + g * FB, FB, 128)], so.at[g, i]) for i in range(n)]
        return [pltpu.make_async_copy(fin.at[g], o_s.at[ds(g * FB, FB, 16)], so.at[g, 0])]

    def cot_rhs(cols):
        return cot[:, :, cols].reshape(RT, 256)

    for k in list(range(1, Z)) + [0]:
        dw_compute(S, k, lambda c0: hact[:, ds(c0, 256, 256)], cot_rhs)

    ag_wait(S)
    hgrad = b.hgrad

    def down(g, acc):
        def step(i, _):
            cols = ds(i * TN, TN, 256)
            rows = ds(g * R, R, 256)
            v = dot_nt(cot[g], ws[cols, :]) * dgelu[rows, cols].astype(F32)
            hgrad[rows, cols] = v.astype(BF)
            return 0
        lax.fori_loop(0, F // TN, step, 0)
        return acc

    lax.fori_loop(0, T, down, 0)
    rs_start(0, 1, hgrad, we, True)
    dw_send(S, 1)

    for k in list(range(1, Z)) + [0]:
        dw_compute(E, k, lambda c0: n2[:, :, ds(c0, 256, 256)].reshape(RT, 256), lambda cols: hgrad[:, cols])
    dw_send(S, 2) if Z > 2 else None

    rs_wait(0, 1)
    proj, fgrad = b.proj, b.fgrad

    def ln2_back(i, carry):
        ag_, as_, ab_ = carry
        rows = ds(i * RB, RB, RB)
        two = rs_value(0, rows)
        nn, sd = norm_parts(first[rows, :])
        e = two * vf[5:6, :]
        og = cot[t, rows, :].astype(F32)
        fg = og + sd * (e - jnp.mean(e, axis=-1, keepdims=True)
                        - nn * jnp.mean(e * nn, axis=-1, keepdims=True))
        fgrad[rows, :] = fg
        pj = fg.astype(BF)
        proj[t, rows, :] = pj
        return (ag_ + jnp.sum(two * nn, axis=0, keepdims=True),
                as_ + jnp.sum(two, axis=0, keepdims=True),
                ab_ + jnp.sum(pj.astype(F32), axis=0, keepdims=True))

    zrow = jnp.zeros((1, D), F32)
    g2, s2, ob = lax.fori_loop(0, nrb, ln2_back, (zrow, zrow, zrow))
    tp_send(proj, b.tproj)
    vg[5:6, :] = g2
    vg[6:7, :] = s2
    vg[4:5, :] = ob
    rs_done(0, 1)

    rs_start(1, 2, hact, ws, False)

    def hb_step(i, _):
        cols = ds(i * TN, TN, 256)
        vgh[0:1, cols] = jnp.sum(hgrad[:, cols].astype(F32), axis=0, keepdims=True)
        return 0
    lax.fori_loop(0, F // TN, hb_step, 0)
    dw_send(S, 3) if Z > 3 else None

    mgrad, jgrad, wo = b.mgrad, b.jgrad, b.w[O]

    def mixed_back(g):
        def step(i, _):
            cols = ds(i * TN, TN, 256)
            mgrad[ds(g * R, R, 256), cols] = dot_nt(proj[g], wo[cols, :]).astype(BF)
            return 0
        lax.fori_loop(0, DT // TN, step, 0)

    def attend_back(g):
        rows = ds(g * R, R, 256)
        for a in range(DT // AW):
            qa = qkv[rows, pl.ds(a * AW, AW)]
            ka = qkv[rows, pl.ds(DT + a * AW, AW)]
            va = qkv[rows, pl.ds(2 * DT + a * AW, AW)]
            ma = mgrad[rows, pl.ds(a * AW, AW)]
            aq = ak = av = None
            for h in range(GH):
                mh = hm(ma, h)
                pg = dot_nt(mh, va)
                pl_ = prob[g * H + a * GH + h]
                p = pl_.astype(F32)
                inner = jnp.sum(p * pg, axis=-1, keepdims=True)
                sg = (p * (pg - inner)).astype(BF)
                dq = dot_nn(sg, hm(ka, h))
                dk = dot_tn(sg, hm(qa, h))
                dv = dot_tn(pl_, mh)
                aq = dq if aq is None else aq + dq
                ak = dk if ak is None else ak + dk
                av = dv if av is None else av + dv
            jgrad[rows, pl.ds(a * AW, AW)] = (aq * scale).astype(BF)
            jgrad[rows, pl.ds(DT + a * AW, AW)] = (ak * scale).astype(BF)
            jgrad[rows, pl.ds(2 * DT + a * AW, AW)] = av.astype(BF)

    rs_wait(1, 2)
    obuf = b.obuf

    def out_step(i, _):
        rows = ds(i * RB, RB, RB)
        r0 = i * RB
        v = (first[rows, :] + rs_value(1, rows) + vf[7:8, :]) * live_of(own_ends, r0, RB)
        obuf[rows, :] = v.astype(BF)
        return 0
    lax.fori_loop(0, nrb, out_step, 0)
    cp_out = pltpu.make_async_copy(obuf, o_out, loc.at[0])
    cp_out.start()

    for g, arrive in order:
        if arrive is not None:
            arrive(proj, b.tproj)
        mixed_back(g)

    for zz in range(ZT):
        dw_compute(O, zz, lambda c0: mixed[:, ds(c0, 256, 256)],
                   lambda cols: proj[:, :, cols].reshape(RT, 256))

    def attb_step(g, _):
        attend_back(g)
        return 0
    lax.fori_loop(0, T // 2, attb_step, 0)
    dw_send(S, 0)
    dw_send(E, 1)
    lax.fori_loop(T // 2, T, attb_step, 0)
    dw_send(E, 2) if Z > 2 else None

    for k in list(range(1, Z)) + [0]:
        dw_compute(J, k, lambda c0: n1[:, ds(c0, 256, 256)], lambda cols: jgrad[:, cols])
    rs_start(0, 3, jgrad, wj, True)
    dw_send(E, 3) if Z > 3 else None
    dw_send(E, 0)
    dw_final(S)
    for i in range(2):
        j = 2 * i
        vg[2 + i:3 + i, ds(t * DT, DT, 128)] = jnp.sum(
            jgrad[:, pl.ds(j * DT, DT)].astype(F32), axis=0, keepdims=True)
    dwo_send()

    rs_wait(0, 3)
    tbuf = b.tbuf

    def ln1_back(i, carry):
        ag_, as_ = carry
        rows = ds(i * RB, RB, RB)
        one = rs_value(0, rows)
        nn, sd = norm_parts(tok[t, rows, :].astype(F32))
        e = one * vf[0:1, :]
        v = fgrad[rows, :] + sd * (e - jnp.mean(e, axis=-1, keepdims=True)
                                   - nn * jnp.mean(e * nn, axis=-1, keepdims=True))
        tbuf[rows, :] = v.astype(BF)
        return (ag_ + jnp.sum(one * nn, axis=0, keepdims=True),
                as_ + jnp.sum(one, axis=0, keepdims=True))

    g1, s1 = lax.fori_loop(0, nrb, ln1_back, (zrow, zrow))
    cp_tg = pltpu.make_async_copy(tbuf, o_tg, loc.at[1])
    cp_tg.start()
    vg[0:1, :] = g1
    vg[1:2, :] = s1

    v3, v3c = b.v3, b.v3c
    kk = FB // Dn
    v3[...] = jnp.zeros_like(v3)
    for i in range(n):
        v3[i, 0:8, :] = vg[:, i * Dn:(i + 1) * Dn]
        for r in range(kk):
            row = vgh[0:1, i * FB + r * Dn:i * FB + (r + 1) * Dn]
            for g in range(T):
                v3[i, 8 + g * kk + r:9 + g * kk + r, :] = jnp.where(t == g, row, jnp.zeros_like(row))
    vt = [rc(v3, v3c.at[0], b.svt[0].at[0], b.svt[1].at[0], core)]
    vt[0].start()
    vt[0].wait()
    v3[...] = v3[...] + v3c[0]
    if X == 2:
        vx = rc(v3, v3c.at[1], b.svt[0].at[1], b.svt[1].at[1], xpeer)
        vx.start()
        vx.wait()
        v3[...] = v3[...] + v3c[1]
    v3y, v3s, v3z = b.v3y, b.v3s, b.v3z

    def vy(m, k):
        return rc(v3.at[zid[k] * Y + yid[m]], v3y.at[m - 1, zid[k]], b.svy[0].at[m - 1, zid[k]],
                  b.svy[1].at[m - 1, zid[k]], ypeer[m])
    for k in range(Z):
        for m in range(1, Y):
            go(vy(m, k))

    dw_send(J, 1)

    def vz(k):
        return rc(v3s.at[k], v3z.at[k - 1], b.svz[0].at[k - 1], b.svz[1].at[k - 1], zpeer[k])
    for k in list(range(1, Z)) + [0]:
        v = v3[zid[k] * Y + y]
        for m in range(1, Y):
            vy(m, k).wait_recv()
            v = v + v3y[m - 1, zid[k]]
        v3s[k] = v
        if k:
            go(vz(k))

    for k in range(2, Z):
        dw_send(J, k)
    dw_send(J, 0)

    copies = []

    def emit(w, g):
        for cp in out_copies(w, g):
            cp.start()
            copies.append(cp)

    dw_final(E)

    @pl.when(mine)
    def _():
        dw_final(O)
        for i, dev in enumerate(peers):
            rc(b.fin[O].at[0], b.fin[O].at[0], b.tfo[0].at[i], b.tfo[1].at[0], dev).start()

    for w in (S, E):
        emit(w, t)
        tp_core(b.fin[w], b.tfin[w])
        emit(w, tc)
        tp_x(b.fin[w], b.tfin[w])
        if X == 2:
            emit(w, tx)

    v = v3s[0]
    for k in range(1, Z):
        vz(k).wait_recv()
        v = v + v3z[k - 1]
    b.vout[...] = v
    cp_v = pltpu.make_async_copy(b.vout, o_vec, loc.at[2])
    cp_v.start()

    dw_final(J)
    for w in (S, E):
        tp_last(b.fin[w], b.tfin[w])
        if X == 2:
            emit(w, txc)

    @pl.when(jnp.logical_not(mine))
    def _():
        rc(b.fin[O].at[0], b.fin[O].at[0], b.tfo[0].at[0], b.tfo[1].at[0], core).wait_recv()
    cp_o = pltpu.make_async_copy(b.fin[O].at[0], o_o, loc.at[3])
    cp_o.start()
    w = J
    emit(w, t)
    tp_core(b.fin[w], b.tfin[w])
    emit(w, tc)
    tp_x(b.fin[w], b.tfin[w])
    tp_last(b.fin[w], b.tfin[w])
    if X == 2:
        emit(w, tx)
        emit(w, txc)

    for cp in pending:
        cp.wait_send()
    for u, r in ((1, 2), (0, 3)):
        rs_done(u, r)
    wo_drain()
    dwo_send(drain=True)

    @pl.when(mine)
    def _():
        for i, dev in enumerate(peers):
            rc(b.fin[O].at[0], b.fin[O].at[0], b.tfo[0].at[i], b.tfo[1].at[0], dev).wait_send()
    for cp in copies + [cp_out, cp_tg, cp_v, cp_o]:
        cp.wait()


def finish(divisor, q, *refs):
    ins, outs = refs[:7], refs[7:]
    for i in range(2):
        outs[i][...] = ins[i][...]
    for i in range(2, 6):
        outs[i][...] = ins[i][...].astype(F32) * (1.0 / divisor)

    @pl.when(pl.program_id(0) == 0)
    def _():
        v = ins[6][...] * (1.0 / divisor)
        for i in range(8):
            outs[6 + i][...] = v[i]
        for r in range(q.FF // q.D):
            outs[14][pl.ds(r * q.Dn, q.Dn)] = v[8 + r]


def body(n_dp, n_fsdp, tokens, patch_counts, gain_one, shift_one, joint_w, query_b, value_b, out_w,
         out_b, gain_two, shift_two, expand_w, expand_b, shrink_w, shrink_b, cotangent):
    R, D = tokens.shape
    q = Sizes(n_dp, n_fsdp, R, D, expand_w.shape[1], patch_counts.shape[1])
    q.grads = [(q.Z, q.Dn, 3 * q.DT), (q.ZT, q.Dn, D), (q.Z, q.Dn, q.F), (q.Z, q.FB, D)]
    scratch, tree = jax.tree.flatten(layout(q))
    anyspec = pl.BlockSpec(memory_space=pl.ANY)
    vmem = pl.BlockSpec(memory_space=pltpu.VMEM)
    sds = jax.ShapeDtypeStruct
    outs = pl.pallas_call(
        functools.partial(kernel, q, tree),
        out_shape=(
            sds((R, D), BF), sds((R, D), BF), sds((VROWS, q.Dn), F32),
            sds((q.Dn, 3 * D), BF), sds((q.Dn, D), BF), sds((q.Dn, q.FF), BF),
            sds((q.FF // q.n, D), BF)),
        in_specs=[anyspec, pl.BlockSpec(memory_space=pltpu.SMEM)] + [anyspec] * 5 + [vmem] * 9,
        out_specs=tuple([anyspec] * 7),
        scratch_shapes=scratch,
        compiler_params=pltpu.CompilerParams(
            collective_id=0, has_side_effects=True, vmem_limit_bytes=67043328),
        name="layer",
    )(tokens, patch_counts, joint_w, out_w, expand_w, shrink_w, cotangent,
      gain_one, shift_one, query_b, value_b, out_b, gain_two, shift_two, shrink_b, expand_b)
    result, tokens_grad, vec, gj, go_, ge, gs = outs
    divisor = float(n_dp * n_fsdp)
    mats = [gj, go_, ge, gs]
    if n_dp > q.T:
        groups = [[i + q.T * g for g in range(n_dp // q.T)] for i in range(q.T)]
        summed = lax.psum(tuple([vec] + mats), "dp", axis_index_groups=groups)
        vec, mats = summed[0], list(summed[1:])
    steps = 4
    blocked = lambda v: pl.BlockSpec((v.shape[0] // steps, v.shape[1]), lambda i: (i, 0))
    rows_in = [result, tokens_grad] + mats
    small = [q.Dn] * 8 + [q.FF // q.n]
    done = pl.pallas_call(
        functools.partial(finish, divisor, q),
        grid=(steps,),
        out_shape=tuple([sds(v.shape, BF) for v in rows_in[:2]] + [sds(v.shape, F32) for v in mats]
                        + [sds((k,), F32) for k in small]),
        in_specs=[blocked(v) for v in rows_in] + [vmem],
        out_specs=tuple([blocked(v) for v in rows_in] + [vmem] * 9),
        name="finish",
    )(*rows_in, vec)
    result, tokens_grad, gj, go_, ge, gs = done[:6]
    vec = done[6:]
    return (result, tokens_grad, vec[0], vec[1], gj, vec[2], vec[3], go_, vec[4], vec[5], vec[6],
            ge, vec[8], gs, vec[7])


def solution(mesh):
    rows = P(("dp", "fsdp"), None)
    vec, mat = P("fsdp"), P("fsdp", None)
    in_specs = (rows, rows, vec, vec, mat, vec, vec, mat, vec, vec, vec, mat, vec, mat, vec, rows)
    out_specs = (rows, rows, vec, vec, mat, vec, vec, mat, vec, vec, vec, mat, vec, mat, vec)
    fn = functools.partial(body, mesh.shape["dp"], mesh.shape["fsdp"])
    return jax.shard_map(fn, mesh=mesh, in_specs=in_specs, out_specs=out_specs, check_vma=False)
```

```python
import functools
from types import SimpleNamespace

import jax
import jax.numpy as jnp
from jax import lax
from jax.experimental import pallas as pl
from jax.experimental.pallas import tpu as pltpu
from jax.sharding import PartitionSpec as P

HEADS = 16
EPS = 1e-05
MASKED = -1e30
MESH = pl.DeviceIdType.MESH
BF = jnp.bfloat16
F32 = jnp.float32
VROWS = 16
J, O, E, S, VEC = range(5)


class Sizes:
    def __init__(self, n_dp, n_fsdp, rows, width, hidden, slots):
        self.n_dp, self.n = n_dp, n_fsdp
        self.R, self.D, self.FF, self.slots = rows, width, hidden, slots
        self.Y = 2 ** ((n_fsdp.bit_length() - 1) // 2)
        self.Z = n_fsdp // self.Y
        T = 4 if n_dp % 4 == 0 else 2
        while hidden // n_fsdp // T % 128 or self.Z % T:
            T //= 2
        self.T, self.X = T, T // 2
        self.RT = T * rows
        self.Dn = width // n_fsdp
        self.DT = width // T
        self.H = HEADS // T
        self.hd = width // HEADS
        self.F = hidden // T
        self.FB = hidden // n_fsdp // T
        self.ZT = self.Z // T


def dot_nn(a, b):
    return jnp.dot(a, b, preferred_element_type=F32)


def dot_nt(a, b):
    return lax.dot_general(a, b, (((1,), (1,)), ((), ())), preferred_element_type=F32)


def dot_tn(a, b):
    return lax.dot_general(a, b, (((0,), (0,)), ((), ())), preferred_element_type=F32)


def ds(start, size, mult):
    return pl.ds(pl.multiple_of(start, mult), size)


def flip(v, k):
    r, bit = v, 1
    while bit <= k:
        if k & bit:
            r = r + bit - 2 * bit * (v // bit % 2)
        bit *= 2
    return r


def norm_parts(x):
    mean = jnp.mean(x, axis=-1, keepdims=True)
    xc = x - mean
    var = jnp.mean(xc * xc, axis=-1, keepdims=True)
    s = lax.rsqrt(var + EPS)
    return xc * s, s


def layout(q):
    R, D, T, RT = q.R, q.D, q.T, q.RT
    Cj = 3 * q.DT
    DMA = pltpu.SemaphoreType.DMA
    V = pltpu.VMEM
    m = SimpleNamespace()
    m.tok = V((T, R, D), BF)
    m.n1 = V((RT, D), BF)
    m.cot = V((T, R, D), BF)
    m.w = [V((D, Cj), BF), V((q.DT, D), BF), V((D, q.F), BF), V((q.F, D), BF)]
    m.qkv = V((RT, Cj), BF)
    m.prob = V((T * q.H, R, R), BF)
    m.mixed = V((RT, q.DT), BF)
    m.first = V((R, D), F32)
    m.n2 = V((T, R, D), BF)
    m.hact = V((RT, q.F), BF)
    m.dgelu = V((RT, q.F), BF)
    m.hgrad = V((RT, q.F), BF)
    m.proj = V((T, R, D), BF)
    m.fgrad = V((R, D), F32)
    m.mgrad = V((RT, q.DT), BF)
    m.jgrad = V((RT, Cj), BF)
    m.acc0 = V((R, D), F32)
    m.psend = [V((q.X, R, D), BF) for _ in range(2)]
    m.precv = [V((q.X, R, D), BF) for _ in range(2)]
    m.xsend = [V((R, D) if q.X == 2 else (16, 128), BF) for _ in range(2)]
    m.xrecv = [V((R, D) if q.X == 2 else (16, 128), BF) for _ in range(2)]
    m.rs = [[DMA((q.X,)), DMA((q.X,)), DMA((1,)), DMA((1,))] for _ in range(4)]
    m.dw = [V((bz, q.Y * rb, C), BF) for bz, rb, C in q.grads]
    m.yr = [V((q.Y - 1, bz, rb, C), BF) for bz, rb, C in q.grads]
    m.zr = [V((q.Z - 1, rb, C), BF) for bz, rb, C in q.grads]
    m.zq = [V((16, 128) if w == O else (rb, C), BF) for w, (bz, rb, C) in enumerate(q.grads)]
    m.fin = [V((1 if w == O else T, rb, C), BF) for w, (bz, rb, C) in enumerate(q.grads)]
    m.sy = [[DMA((q.Y - 1, bz)), DMA((q.Y - 1, bz))] for bz, rb, C in q.grads]
    m.sz = [[DMA((q.Z - 1,)), DMA((q.Z,))] for _ in q.grads]
    m.sout = [DMA((T, q.n)) for _ in q.grads]
    m.gz = [[DMA((q.Z,)), DMA((max(q.Z - 1, q.ZT),))] for _ in range(5)]
    m.gy = [[DMA((q.Y - 1, q.Z)), DMA((q.Y - 1, q.Z))] for _ in range(5)]
    pair = lambda: [DMA((3,)), DMA((3,))]
    m.ttok, m.tcot, m.tn2, m.tproj, m.tcnt, m.tfo = (pair() for _ in range(6))
    m.tfin = [pair() for _ in q.grads]
    m.vec = V((q.n, VROWS, q.Dn), BF)
    m.vf = V((8, D), F32)
    m.hb = V((8, q.F), F32)
    m.cnt = V((T, 8, 128), jnp.int32)
    m.vg = V((8, D), F32)
    m.vgh = V((8, q.F), F32)
    m.v3 = V((q.n, VROWS, q.Dn), F32)
    m.v3c = V((2, q.n, VROWS, q.Dn), F32)
    m.v3y = V((q.Y - 1, q.Z, VROWS, q.Dn), F32)
    m.v3s = V((q.Z, VROWS, q.Dn), F32)
    m.v3z = V((q.Z - 1, VROWS, q.Dn), F32)
    m.vout = V((VROWS, q.Dn), F32)
    m.svt = [DMA((2,)), DMA((2,))]
    m.svy = [DMA((q.Y - 1, q.Z)), DMA((q.Y - 1, q.Z))]
    m.svz = [DMA((q.Z - 1,)), DMA((q.Z - 1,))]
    m.loc = DMA((7 + q.n,))
    return vars(m)


def kernel(q, tree, *refs):
    (tokens, counts, joint_w, out_w, exp_w, shr_w, cotangent) = refs[:7]
    vectors = refs[7:16]
    (o_out, o_tg, o_vec, o_j, o_o, o_e, o_s) = refs[16:23]
    b = SimpleNamespace(**jax.tree.unflatten(tree, refs[23:]))
    R, D, T, X, RT, n, Y, Z = q.R, q.D, q.T, q.X, q.RT, q.n, q.Y, q.Z
    Dn, DT, F, FB, H, hd, ZT = q.Dn, q.DT, q.F, q.FB, q.H, q.hd, q.ZT
    Cj = 3 * DT

    dp = lax.axis_index("dp")
    s = lax.axis_index("fsdp")
    t = dp % T
    c, xx = t % 2, t // 2
    y, z = s % Y, s // Y
    core = (dp + 1 - 2 * c, s)
    xdp = dp + 2 - 4 * xx
    xpeer = (xdp, s)
    xcore = (xdp + 1 - 2 * c, s)
    tc = t + 1 - 2 * c
    if X == 2:
        tx = t + 2 - 4 * xx
        txc = tx + 1 - 2 * c
    zid = [flip(z, k) for k in range(Z)]
    relay = Z == 4
    inner = jnp.logical_and(z > 0, z < Z - 1)
    outer = jnp.logical_not(inner)
    zfar = jnp.where(z > 1, Z - 1, 0)
    yid = [(y + k) % Y for k in range(Y)]
    ysrc = [(y + Y - k) % Y for k in range(Y)]
    zpeer = [(dp, zid[k] * Y + y) for k in range(Z)]
    ypeer = [(dp, z * Y + yid[k]) for k in range(Y)]
    pending, pending_if = [], []

    def rc(src, dst, ss, rs, dev):
        return pltpu.make_async_remote_copy(
            src_ref=src, dst_ref=dst, send_sem=ss, recv_sem=rs,
            device_id=dev, device_id_type=MESH)

    def go(cp):
        cp.start()
        pending.append(cp)
        return cp

    def go_if(pred, cp):
        pl.when(pred)(cp.start)
        pending_if.append((pred, cp))

    loc = b.loc
    cp_tok = pltpu.make_async_copy(tokens, b.tok.at[t], loc.at[0])
    cp_cot = pltpu.make_async_copy(cotangent, b.cot.at[t], loc.at[1])
    cp_shr = pltpu.make_async_copy(
        shr_w.at[ds(t * FB, FB, 16)], b.w[S].at[ds(s * FB, FB, 16)], loc.at[3])
    cp_j = [pltpu.make_async_copy(
        joint_w.at[:, ds(j * D + t * DT, DT, 128)],
        b.w[J].at[ds(s * Dn, Dn, 16), pl.ds(j * DT, DT)], loc.at[4 + j]) for j in range(3)]
    cp_e = [pltpu.make_async_copy(
        exp_w.at[:, ds(i * (T * FB) + t * FB, FB, 128)],
        b.w[E].at[ds(s * Dn, Dn, 16), pl.ds(i * FB, FB)], loc.at[7 + i]) for i in range(n)]
    for cp in cp_j + [cp_tok] + cp_e + [cp_shr, cp_cot]:
        cp.start()

    lane = lax.broadcasted_iota(jnp.int32, (8, 128), 1)
    cv = jnp.zeros((8, 128), jnp.int32)
    for i in range(q.slots):
        cv = jnp.where(lane == i, counts[0, i], cv)
    b.cnt[t] = cv

    bar = pltpu.get_barrier_semaphore()
    greet = [core] + ([xpeer, xcore] if X == 2 else []) + zpeer[1:] + ypeer[1:]
    for dev in greet:
        pl.semaphore_signal(bar, inc=1, device_id=dev, device_id_type=MESH)
    pl.semaphore_wait(bar, len(greet))

    def slot(w, src_s):
        if w == VEC:
            return b.vec.at[src_s]
        if w == S:
            return b.w[S].at[ds(src_s * FB, FB, 16)]
        return b.w[w].at[ds(src_s * Dn, Dn, 16)]

    def gz_copy(w, k):
        return rc(slot(w, s), slot(w, s), b.gz[w][0].at[k - 1], b.gz[w][1].at[k - 1], zpeer[k])

    def gz_wait(w, k):
        src = slot(w, zid[k] * Y + y)
        rc(src, src, b.gz[w][0].at[k - 1], b.gz[w][1].at[k - 1], zpeer[k]).wait_recv()

    def gy_copies(w, k):
        src = slot(w, zid[k] * Y + y)
        return [rc(src, src, b.gy[w][0].at[m - 1, k], b.gy[w][1].at[m - 1, k], ypeer[m])
                for m in range(1, Y)]

    def ag_z(w):
        if not relay or w == VEC:
            for k in range(1, Z):
                go(gz_copy(w, k))
            return
        go(gz_copy(w, 1))
        go_if(inner, gz_copy(w, 3))
        go(gz_copy(w, 2))

    def ag_y(w, k):
        if k:
            gz_wait(w, k)
        if relay and w != VEC and k == 2:
            src = slot(w, zid[k] * Y + y)
            go_if(inner, rc(src, src, b.gz[w][0].at[Z - 1], b.gz[w][1].at[2], (dp, zfar * Y + y)))
        for cp in gy_copies(w, k):
            go(cp)

    def ag_y_if(pred, w, k):
        @pl.when(pred)
        def _():
            gz_wait(w, k)
            for cp in gy_copies(w, k):
                cp.start()

    def fw(w, *steps):
        for i in steps:
            if not relay or w == VEC:
                if i < Z:
                    ag_y(w, i)
            elif i == 2:
                ag_y_if(inner, w, 3)
            elif i == 4:
                ag_y_if(outer, w, 3)
                pending.extend(gy_copies(w, 3))
            else:
                ag_y(w, {0: 0, 1: 1, 3: 2}[i])

    def ag_wait(w):
        for k in range(Z):
            for m in range(1, Y):
                src = zid[k] * Y + ysrc[m]
                rc(slot(w, src), slot(w, src), b.gy[w][0].at[m - 1, k], b.gy[w][1].at[m - 1, k], ypeer[m]).wait_recv()

    zlo = t * ZT
    mine = z // ZT == t

    def wo_slot(zz, yy):
        return b.w[O].at[ds((zz * Y + yy) * Dn, Dn, 16)]

    def wo_z():
        @pl.when(mine)
        def _():
            zz = z - zlo
            for k in range(1, Z):
                rc(out_w, wo_slot(zz, y), b.gz[O][0].at[k - 1], b.gz[O][1].at[zz], zpeer[k]).start()
            pltpu.make_async_copy(out_w, wo_slot(zz, y), b.gz[O][1].at[zz]).start()

    def wo_y():
        for zz in range(ZT):
            pltpu.make_async_copy(out_w, wo_slot(zz, y), b.gz[O][1].at[zz]).wait()
            for m in range(1, Y):
                go(rc(wo_slot(zz, y), wo_slot(zz, y), b.gy[O][0].at[m - 1, zz], b.gy[O][1].at[m - 1, zz], ypeer[m]))

    def wo_wait():
        for zz in range(ZT):
            for m in range(1, Y):
                rc(wo_slot(zz, ysrc[m]), wo_slot(zz, ysrc[m]), b.gy[O][0].at[m - 1, zz], b.gy[O][1].at[m - 1, zz], ypeer[m]).wait_recv()

    def wo_drain():
        @pl.when(mine)
        def _():
            for k in range(1, Z):
                rc(out_w, wo_slot(z - zlo, y), b.gz[O][0].at[k - 1], b.gz[O][1].at[0], zpeer[k]).wait_send()

    def tp_send(buf, w, src=None):
        src = buf.at[t] if src is None else src
        if X == 2:
            go(rc(src, buf.at[t], w[0].at[1], w[1].at[1], xpeer))
        go(rc(src, buf.at[t], w[0].at[0], w[1].at[0], core))

    def tp_core(buf, w):
        rc(buf.at[tc], buf.at[tc], w[0].at[0], w[1].at[0], core).wait_recv()

    def tp_x(buf, w):
        if X == 2:
            rc(buf.at[tx], buf.at[tx], w[0].at[1], w[1].at[1], xpeer).wait_recv()
            go(rc(buf.at[tx], buf.at[tx], w[0].at[2], w[1].at[2], core))

    def tp_last(buf, w):
        if X == 2:
            rc(buf.at[txc], buf.at[txc], w[0].at[2], w[1].at[2], core).wait_recv()

    order = [(t, None), (tc, tp_core)] + ([(tx, tp_x), (txc, tp_last)] if X == 2 else [])

    vrow = lax.broadcasted_iota(jnp.int32, (VROWS, Dn), 0)
    packed = jnp.zeros((VROWS, Dn), F32)
    pieces = [v[...] for v in vectors[:8]]
    pieces += [vectors[8][pl.ds(r * Dn, Dn)] for r in range(vectors[8].shape[0] // Dn)]
    for i, piece in enumerate(pieces):
        packed = jnp.where(vrow == i, piece.astype(F32).reshape(1, Dn), packed)
    b.vec[s] = packed.astype(BF)
    ag_z(VEC)
    ag_y(VEC, 0)
    cnt = b.cnt
    peers = [core] + ([xpeer, xcore] if X == 2 else [])
    for i, dev in enumerate(peers):
        go(rc(cnt.at[t], cnt.at[t], b.tcnt[0].at[i], b.tcnt[1].at[i], dev))
    for cp in cp_j:
        cp.wait()
    ag_z(J)
    fw(J, 0)
    cp_tok.wait()
    tp_send(b.tok, b.ttok)
    wo_z()
    last = range(4, max(Z, 5))

    fw(VEC, *range(1, Z))
    ag_wait(VEC)
    vf, hb = b.vf, b.hb
    for i in range(n):
        piece = b.vec[i].astype(F32)
        vf[:, i * Dn:(i + 1) * Dn] = piece[0:8]
        kk = FB // Dn
        for r in range(kk):
            row = piece[8 + r:9 + r]
            for g in range(1, T):
                row = jnp.where(t == g, piece[8 + g * kk + r:9 + g * kk + r], row)
            hb[0:1, i * FB + r * Dn:i * FB + (r + 1) * Dn] = row
    vg, vgh = b.vg, b.vgh
    vg[...] = jnp.zeros_like(vg)

    for i, st in enumerate([tc] + ([tx, txc] if X == 2 else [])):
        rc(cnt.at[st], cnt.at[st], b.tcnt[0].at[i], b.tcnt[1].at[i], peers[i]).wait_recv()

    def ends_of(g):
        row = cnt[g]
        ends, total = [], None
        for i in range(q.slots):
            v = row[0:1, i:i + 1]
            total = v if total is None else total + v
            ends.append(total)
        return ends

    RB = 64
    nrb = R // RB

    def live_of(ends, r0, rows):
        places = lax.broadcasted_iota(jnp.int32, (rows, 1), 0) + r0
        return (places < ends[-1]).astype(F32)

    own_ends = ends_of(t)
    cp_cot.wait()
    cot = b.cot

    def cot_step(i, acc):
        r0 = pl.multiple_of(i * RB, RB)
        v = cot[t, pl.ds(r0, RB), :].astype(F32) * live_of(own_ends, r0, RB)
        cot[t, pl.ds(r0, RB), :] = v.astype(BF)
        return acc + jnp.sum(v, axis=0, keepdims=True)

    vg[7:8, :] = lax.fori_loop(0, nrb, cot_step, jnp.zeros((1, D), F32))
    tp_send(cot, b.tcot)

    tok, n1 = b.tok, b.n1

    def ln1(g):
        def step(i, _):
            r0 = pl.multiple_of(i * RB, RB)
            nn, _s = norm_parts(tok[g, pl.ds(r0, RB), :].astype(F32))
            n1[ds(g * R + r0, RB, RB), :] = (nn * vf[0:1, :] + vf[1:2, :]).astype(BF)
            return 0
        lax.fori_loop(0, nrb, step, 0)

    ln1(t)
    tp_core(tok, b.ttok)
    ln1(tc)
    fw(J, 1)
    tp_x(tok, b.ttok)
    fw(J, 2)
    if X == 2:
        ln1(tx)
        tp_last(tok, b.ttok)
        ln1(txc)
    fw(J, 3)
    fw(J, *last)
    for cp in cp_e:
        cp.wait()
    ag_z(E)
    fw(E, 0)
    ag_wait(J)

    qkv, wj = b.qkv, b.w[J]
    TN = 256
    for j in range(3):
        def step(i, _, j=j):
            col = j * DT + i * TN
            r = dot_nn(n1[...], wj[:, ds(col, TN, 128)])
            if j != 1:
                r = r + vf[(2 if j == 0 else 3):(3 if j == 0 else 4), ds(t * DT + i * TN, TN, 128)]
            qkv[:, ds(col, TN, 128)] = r.astype(BF)
            return 0
        lax.fori_loop(0, DT // TN, step, 0)

    scale = hd ** (-0.5)
    prob, mixed = b.prob, b.mixed
    AW = 256
    GH = AW // hd
    lanes = lax.broadcasted_iota(jnp.int32, (1, AW), 1)
    head_masks = [(lanes // hd == h) for h in range(GH)]

    def hm(v, h):
        return jnp.where(head_masks[h], v, jnp.zeros_like(v))

    def attend(g):
        ends = ends_of(g)
        ri = lax.broadcasted_iota(jnp.int32, (R, R), 0)
        ci = lax.broadcasted_iota(jnp.int32, (R, R), 1)
        im_r = jnp.zeros((R, R), jnp.int32)
        im_c = jnp.zeros((R, R), jnp.int32)
        for e in ends:
            im_r = im_r + (ri >= e).astype(jnp.int32)
            im_c = im_c + (ci >= e).astype(jnp.int32)
        same = im_r == im_c
        rows = ds(g * R, R, 256)
        for a in range(DT // AW):
            qa = qkv[rows, pl.ds(a * AW, AW)]
            ka = qkv[rows, pl.ds(DT + a * AW, AW)]
            va = qkv[rows, pl.ds(2 * DT + a * AW, AW)]
            acc = None
            for h in range(GH):
                sc = dot_nt(hm(qa, h), ka) * scale
                sc = jnp.where(same, sc, MASKED)
                top = jnp.max(sc, axis=-1, keepdims=True)
                ex = jnp.exp(sc - top)
                tot = jnp.sum(ex, axis=-1, keepdims=True)
                p = (ex * (1.0 / tot)).astype(BF)
                prob[g * H + a * GH + h] = p
                part = dot_nn(p, hm(va, h))
                acc = part if acc is None else acc + part
            mixed[rows, pl.ds(a * AW, AW)] = acc.astype(BF)

    def att_step(g, _):
        attend(g)
        return 0

    lax.fori_loop(0, T, att_step, 0)
    wo_y()
    cp_shr.wait()
    ag_z(S)
    fw(E, 1)
    wo_wait()

    acc0 = b.acc0

    def block_mm(lhs, g, rhs, nt, put):
        def step(i, _):
            cols = ds(i * TN, TN, 256)
            a = lhs[ds(g * R, R, 256), :]
            put(cols, dot_nt(a, rhs[cols, :]) if nt else dot_nn(a, rhs[:, cols]))
            return 0
        lax.fori_loop(0, D // TN, step, 0)

    def rs_copy(u, r, i):
        return rc(b.psend[u].at[i], b.precv[u].at[i], b.rs[r][0].at[i], b.rs[r][1].at[i], core)

    def rs_xcopy(u, r):
        return rc(b.xsend[u], b.xrecv[u], b.rs[r][2].at[0], b.rs[r][3].at[0], xpeer)

    def rs_start(u, r, lhs, rhs, nt):
        ps = b.psend[u]

        def put_at(i):
            def put(cols, v):
                ps[i, :, cols] = v.astype(BF)
            return put

        def put_acc(cols, v):
            acc0[:, cols] = v

        if X == 2:
            block_mm(lhs, txc, rhs, nt, put_at(1))
            rs_copy(u, r, 1).start()
            block_mm(lhs, tx, rhs, nt, put_acc)
            rs_copy(u, r, 1).wait_recv()
            pr, xs = b.precv[u], b.xsend[u]

            def add(i, _):
                rows = ds(i * RB, RB, RB)
                xs[rows, :] = (acc0[rows, :] + pr[1, rows, :].astype(F32)).astype(BF)
                return 0
            lax.fori_loop(0, nrb, add, 0)
            rs_xcopy(u, r).start()
        block_mm(lhs, tc, rhs, nt, put_at(0))
        rs_copy(u, r, 0).start()
        block_mm(lhs, t, rhs, nt, put_acc)

    def rs_wait(u, r):
        rs_copy(u, r, 0).wait_recv()
        if X == 2:
            rs_xcopy(u, r).wait_recv()

    def rs_value(u, rows):
        v = acc0[rows, :] + b.precv[u][0, rows, :].astype(F32)
        if X == 2:
            v = v + b.xrecv[u][rows, :].astype(F32)
        return v

    def rs_done(u, r):
        for i in range(X):
            rs_copy(u, r, i).wait_send()
        if X == 2:
            rs_xcopy(u, r).wait_send()

    rs_start(0, 0, mixed, b.w[O], False)
    tp_core(cot, b.tcot)
    tp_x(cot, b.tcot)
    fw(E, 2)
    fw(E, 3)
    rs_wait(0, 0)
    first, n2 = b.first, b.n2

    def ln2(i, _):
        rows = ds(i * RB, RB, RB)
        v = tok[t, rows, :].astype(F32) + (rs_value(0, rows) + vf[4:5, :])
        first[rows, :] = v
        nn, _s = norm_parts(v)
        n2[t, rows, :] = (nn * vf[5:6, :] + vf[6:7, :]).astype(BF)
        return 0
    lax.fori_loop(0, nrb, ln2, 0)
    tp_send(n2, b.tn2)
    fw(E, *last)
    fw(S, 0)
    rs_done(0, 0)
    tp_last(cot, b.tcot)
    ag_wait(E)

    hact, dgelu, we, ws = b.hact, b.dgelu, b.w[E], b.w[S]

    def up(g):
        def step(i, _):
            cols = ds(i * TN, TN, 256)
            rows = ds(g * R, R, 256)
            h = dot_nn(n2[g], we[:, cols]) + hb[0:1, cols]
            phi = 0.5 * (1.0 + lax.erf(h * 0.7071067811865476))
            hact[rows, cols] = (h * phi).astype(BF)
            dgelu[rows, cols] = (phi + h * (jnp.exp(-0.5 * h * h) * 0.3989422804014327)).astype(BF)
            return 0
        lax.fori_loop(0, F // TN, step, 0)

    up(t)
    tp_core(n2, b.tn2)
    up(tc)
    fw(S, 1)
    tp_x(n2, b.tn2)
    if X == 2:
        up(tx)
        tp_last(n2, b.tn2)
        up(txc)
    fw(S, 2)
    fw(S, 3)
    fw(S, *last)

    def blocks(w):
        return q.grads[w]

    def dw_dest(w, k):
        return zlo + k if w == O else zid[k]

    def dw_slot(w, k):
        return k if w == O else zid[k]

    def dw_y(w, sl, m):
        rb = blocks(w)[1]
        return rc(b.dw[w].at[sl, ds(yid[m] * rb, rb, 16)], b.yr[w].at[m - 1, sl],
                  b.sy[w][0].at[m - 1, sl], b.sy[w][1].at[m - 1, sl], ypeer[m])

    def dw_compute(w, k, lhs, rhs):
        bz, rb, C = blocks(w)
        sl = dw_slot(w, k)
        tile = Y * rb
        TC = 256

        def step(i, _):
            cols = ds(i * TC, TC, 256)
            for r in range(tile // 256):
                a = lhs(sl * tile + r * 256)
                b.dw[w][sl, pl.ds(r * 256, 256), cols] = dot_tn(a, rhs(cols)).astype(BF)
            return 0
        lax.fori_loop(0, C // TC, step, 0)
        for m in range(1, Y):
            go(dw_y(w, sl, m))

    def dw_sum(w, k):
        bz, rb, C = blocks(w)
        sl = dw_slot(w, k)
        for m in range(1, Y):
            dw_y(w, sl, m).wait_recv()
        ch = 64

        def add(i, _):
            rows = ds(y * rb + i * ch, ch, 64)
            v = b.dw[w][sl, rows, :].astype(F32)
            for m in range(1, Y):
                v = v + b.yr[w][m - 1, sl, ds(i * ch, ch, 64), :].astype(F32)
            b.dw[w][sl, rows, :] = v.astype(BF)
            return 0
        lax.fori_loop(0, rb // ch, add, 0)

    def dw_z(w, k):
        rb = blocks(w)[1]
        return rc(b.dw[w].at[zid[k], ds(y * rb, rb, 16)], b.zr[w].at[k - 1],
                  b.sz[w][0].at[k - 1], b.sz[w][1].at[k - 1], zpeer[k])

    def dw_o(zz, k):
        return rc(b.dw[O].at[zz, ds(y * Dn, Dn, 16)], b.zr[O].at[k - 1],
                  b.sz[O][0].at[k - 1], b.sz[O][1].at[k - 1], zpeer[k])

    def dw_relay(w):
        rb = blocks(w)[1]
        return rc(b.dw[w].at[zid[3], ds(y * rb, rb, 16)], b.zq[w], b.sz[w][0].at[2],
                  b.sz[w][1].at[Z - 1], zpeer[1])

    def dw_send(w, k):
        dw_sum(w, k)
        if relay and k == 3:
            go_if(inner, dw_z(w, k))
            go_if(outer, dw_relay(w))
            return
        if relay and k == 2:
            @pl.when(inner)
            def _():
                dw_relay(w).wait_recv()
                rb, ch = blocks(w)[1], 64

                def add(i, _):
                    rows = ds(y * rb + i * ch, ch, 64)
                    v = b.dw[w][zid[2], rows, :].astype(F32) + b.zq[w][ds(i * ch, ch, 64), :].astype(F32)
                    b.dw[w][zid[2], rows, :] = v.astype(BF)
                    return 0
                lax.fori_loop(0, rb // ch, add, 0)
        if k:
            go(dw_z(w, k))

    def dwo_send(drain=False):
        for zz in range(ZT):
            if not drain:
                dw_sum(O, zz)
            for k in range(1, Z):
                @pl.when(zid[k] == zlo + zz)
                def _(zz=zz, k=k):
                    if drain:
                        dw_o(zz, k).wait_send()
                    else:
                        dw_o(zz, k).start()

    def dw_final(w):
        bz, rb, C = blocks(w)
        ch = 64
        fin = b.fin[w]
        own = z - zlo if w == O else z
        me = 0 if w == O else t

        def total(ks):
            for k in ks:
                (dw_o(0, k) if w == O else dw_z(w, k)).wait_recv()

            def add(i, _):
                rows = ds(i * ch, ch, 64)
                v = b.dw[w][own, ds(y * rb + i * ch, ch, 64), :].astype(F32)
                for k in ks:
                    v = v + b.zr[w][k - 1, rows, :].astype(F32)
                fin[me, rows, :] = v.astype(BF)
                return 0
            lax.fori_loop(0, rb // ch, add, 0)

        if relay and w != O:
            pl.when(inner)(lambda: total((1, 2, 3)))
            pl.when(outer)(lambda: total((1, 2)))
        else:
            total(range(1, Z))
        if w != O:
            tp_send(fin, b.tfin[w])

    def out_copies(w, g):
        fin, so = b.fin[w], b.sout[w]
        if w == J:
            return [pltpu.make_async_copy(fin.at[g, :, pl.ds(j * DT, DT)],
                    o_j.at[:, ds(j * D + g * DT, DT, 128)], so.at[g, j]) for j in range(3)]
        if w == E:
            return [pltpu.make_async_copy(fin.at[g, :, pl.ds(i * FB, FB)],
                    o_e.at[:, ds(i * (T * FB) + g * FB, FB, 128)], so.at[g, i]) for i in range(n)]
        return [pltpu.make_async_copy(fin.at[g], o_s.at[ds(g * FB, FB, 16)], so.at[g, 0])]

    def cot_rhs(cols):
        return cot[:, :, cols].reshape(RT, 256)

    zorder = ([3, 1, 2] if relay else list(range(1, Z))) + [0]
    half = len(zorder) // 2

    def dw_shrink(ks):
        for k in ks:
            dw_compute(S, k, lambda c0: hact[:, ds(c0, 256, 256)], cot_rhs)

    dw_shrink(zorder[:half])
    dw_shrink(zorder[half:])
    ag_wait(S)
    hgrad = b.hgrad

    def down(g, acc):
        def step(i, _):
            cols = ds(i * TN, TN, 256)
            rows = ds(g * R, R, 256)
            v = dot_nt(cot[g], ws[cols, :]) * dgelu[rows, cols].astype(F32)
            hgrad[rows, cols] = v.astype(BF)
            return 0
        lax.fori_loop(0, F // TN, step, 0)
        return acc

    lax.fori_loop(0, T, down, 0)
    def send(w, *steps):
        for i in steps:
            if i < Z:
                dw_send(w, zorder[i])

    send(S, 0)
    rs_start(0, 1, hgrad, we, True)
    send(S, 1)

    def dw_expand(ks):
        for k in ks:
            dw_compute(E, k, lambda c0: n2[:, :, ds(c0, 256, 256)].reshape(RT, 256),
                       lambda cols: hgrad[:, cols])

    dw_expand(zorder[:half])
    send(S, 2)
    dw_expand(zorder[half:])
    rs_wait(0, 1)
    proj, fgrad = b.proj, b.fgrad

    def ln2_back(i, carry):
        ag_, as_, ab_ = carry
        rows = ds(i * RB, RB, RB)
        two = rs_value(0, rows)
        nn, sd = norm_parts(first[rows, :])
        e = two * vf[5:6, :]
        og = cot[t, rows, :].astype(F32)
        fg = og + sd * (e - jnp.mean(e, axis=-1, keepdims=True)
                        - nn * jnp.mean(e * nn, axis=-1, keepdims=True))
        fgrad[rows, :] = fg
        pj = fg.astype(BF)
        proj[t, rows, :] = pj
        return (ag_ + jnp.sum(two * nn, axis=0, keepdims=True),
                as_ + jnp.sum(two, axis=0, keepdims=True),
                ab_ + jnp.sum(pj.astype(F32), axis=0, keepdims=True))

    zrow = jnp.zeros((1, D), F32)
    g2, s2, ob = lax.fori_loop(0, nrb, ln2_back, (zrow, zrow, zrow))
    tp_send(proj, b.tproj)
    vg[5:6, :] = g2
    vg[6:7, :] = s2
    vg[4:5, :] = ob
    rs_done(0, 1)

    send(S, *range(3, Z))
    rs_start(1, 2, hact, ws, False)

    def hb_step(i, _):
        cols = ds(i * TN, TN, 256)
        vgh[0:1, cols] = jnp.sum(hgrad[:, cols].astype(F32), axis=0, keepdims=True)
        return 0
    lax.fori_loop(0, F // TN, hb_step, 0)
    mgrad, jgrad, wo = b.mgrad, b.jgrad, b.w[O]

    def mixed_back(g):
        def step(i, _):
            cols = ds(i * TN, TN, 256)
            mgrad[ds(g * R, R, 256), cols] = dot_nt(proj[g], wo[cols, :]).astype(BF)
            return 0
        lax.fori_loop(0, DT // TN, step, 0)

    def attend_back(g):
        rows = ds(g * R, R, 256)
        for a in range(DT // AW):
            qa = qkv[rows, pl.ds(a * AW, AW)]
            ka = qkv[rows, pl.ds(DT + a * AW, AW)]
            va = qkv[rows, pl.ds(2 * DT + a * AW, AW)]
            ma = mgrad[rows, pl.ds(a * AW, AW)]
            aq = ak = av = None
            for h in range(GH):
                mh = hm(ma, h)
                pg = dot_nt(mh, va)
                pl_ = prob[g * H + a * GH + h]
                p = pl_.astype(F32)
                inner = jnp.sum(p * pg, axis=-1, keepdims=True)
                sg = (p * (pg - inner)).astype(BF)
                dq = dot_nn(sg, hm(ka, h))
                dk = dot_tn(sg, hm(qa, h))
                dv = dot_tn(pl_, mh)
                aq = dq if aq is None else aq + dq
                ak = dk if ak is None else ak + dk
                av = dv if av is None else av + dv
            jgrad[rows, pl.ds(a * AW, AW)] = (aq * scale).astype(BF)
            jgrad[rows, pl.ds(DT + a * AW, AW)] = (ak * scale).astype(BF)
            jgrad[rows, pl.ds(2 * DT + a * AW, AW)] = av.astype(BF)

    obuf = n2.at[tc]

    def out_step(i, _):
        rows = ds(i * RB, RB, RB)
        r0 = i * RB
        v = (first[rows, :] + rs_value(1, rows) + vf[7:8, :]) * live_of(own_ends, r0, RB)
        obuf[rows, :] = v.astype(BF)
        return 0
    def attb_step(g, _):
        attend_back(g)
        return 0

    send(E, 0)
    mixed_back(t)
    tp_core(proj, b.tproj)
    mixed_back(tc)
    attend_back(t)
    send(E, 1)
    tp_x(proj, b.tproj)
    attend_back(tc)
    if X == 2:
        mixed_back(tx)
        attend_back(tx)
    tp_last(proj, b.tproj)
    for zz in range(ZT):
        dw_compute(O, zz, lambda c0: mixed[:, ds(c0, 256, 256)],
                   lambda cols: proj[:, :, cols].reshape(RT, 256))
    if X == 2:
        mixed_back(txc)
        attend_back(txc)
    send(E, 2)
    for k in zorder:
        dw_compute(J, k, lambda c0: n1[:, ds(c0, 256, 256)], lambda cols: jgrad[:, cols])
    send(E, *range(3, Z))
    dw_final(S)
    rs_wait(1, 2)
    lax.fori_loop(0, nrb, out_step, 0)
    cp_out = pltpu.make_async_copy(obuf, o_out, loc.at[0])
    cp_out.start()
    rs_start(0, 3, jgrad, wj, True)
    dwo_send()
    send(J, 0)
    for i in range(2):
        j = 2 * i
        vg[2 + i:3 + i, ds(t * DT, DT, 128)] = jnp.sum(
            jgrad[:, pl.ds(j * DT, DT)].astype(F32), axis=0, keepdims=True)
    send(J, 1)

    rs_wait(0, 3)
    tbuf = proj.at[tc]

    def ln1_back(i, carry):
        ag_, as_ = carry
        rows = ds(i * RB, RB, RB)
        one = rs_value(0, rows)
        nn, sd = norm_parts(tok[t, rows, :].astype(F32))
        e = one * vf[0:1, :]
        v = fgrad[rows, :] + sd * (e - jnp.mean(e, axis=-1, keepdims=True)
                                   - nn * jnp.mean(e * nn, axis=-1, keepdims=True))
        tbuf[rows, :] = v.astype(BF)
        return (ag_ + jnp.sum(one * nn, axis=0, keepdims=True),
                as_ + jnp.sum(one, axis=0, keepdims=True))

    g1, s1 = lax.fori_loop(0, nrb, ln1_back, (zrow, zrow))
    cp_tg = pltpu.make_async_copy(tbuf, o_tg, loc.at[1])
    cp_tg.start()
    vg[0:1, :] = g1
    vg[1:2, :] = s1

    v3, v3c = b.v3, b.v3c
    kk = FB // Dn
    v3[...] = jnp.zeros_like(v3)
    for i in range(n):
        v3[i, 0:8, :] = vg[:, i * Dn:(i + 1) * Dn]
        for r in range(kk):
            row = vgh[0:1, i * FB + r * Dn:i * FB + (r + 1) * Dn]
            for g in range(T):
                v3[i, 8 + g * kk + r:9 + g * kk + r, :] = jnp.where(t == g, row, jnp.zeros_like(row))
    vt = rc(v3, v3c.at[0], b.svt[0].at[0], b.svt[1].at[0], core)
    vt.start()
    send(J, 2)
    vt.wait()
    v3[...] = v3[...] + v3c[0]
    if X == 2:
        vx = rc(v3, v3c.at[1], b.svt[0].at[1], b.svt[1].at[1], xpeer)
        vx.start()
        vx.wait()
        v3[...] = v3[...] + v3c[1]
    v3y, v3s, v3z = b.v3y, b.v3s, b.v3z

    def vy(m, k):
        return rc(v3.at[zid[k] * Y + yid[m]], v3y.at[m - 1, zid[k]], b.svy[0].at[m - 1, zid[k]],
                  b.svy[1].at[m - 1, zid[k]], ypeer[m])
    for k in range(Z):
        for m in range(1, Y):
            go(vy(m, k))

    dw_final(E)
    copies = []

    def emit(w, g):
        for cp in out_copies(w, g):
            cp.start()
            copies.append(cp)

    emit(S, t)
    tp_core(b.fin[S], b.tfin[S])
    emit(S, tc)
    tp_x(b.fin[S], b.tfin[S])
    if X == 2:
        emit(S, tx)
    send(J, *range(3, Z))


    def vz(k):
        return rc(v3s.at[k], v3z.at[k - 1], b.svz[0].at[k - 1], b.svz[1].at[k - 1], zpeer[k])
    for k in zorder:
        v = v3[zid[k] * Y + y]
        for m in range(1, Y):
            vy(m, k).wait_recv()
            v = v + v3y[m - 1, zid[k]]
        v3s[k] = v
        if k:
            go(vz(k))

    emit(E, t)
    tp_core(b.fin[E], b.tfin[E])
    emit(E, tc)
    tp_x(b.fin[E], b.tfin[E])
    if X == 2:
        emit(E, tx)
    dw_final(J)

    @pl.when(mine)
    def _():
        dw_final(O)
        for i, dev in enumerate(peers):
            rc(b.fin[O].at[0], b.fin[O].at[0], b.tfo[0].at[i], b.tfo[1].at[0], dev).start()

    v = v3s[0]
    for k in range(1, Z):
        vz(k).wait_recv()
        v = v + v3z[k - 1]
    b.vout[...] = v
    cp_v = pltpu.make_async_copy(b.vout, o_vec, loc.at[2])
    cp_v.start()

    emit(J, t)
    tp_core(b.fin[J], b.tfin[J])
    emit(J, tc)
    tp_x(b.fin[J], b.tfin[J])
    for w in (S, E, J):
        tp_last(b.fin[w], b.tfin[w])
        if X == 2:
            emit(w, txc)
    if X == 2:
        emit(J, tx)

    @pl.when(jnp.logical_not(mine))
    def _():
        rc(b.fin[O].at[0], b.fin[O].at[0], b.tfo[0].at[0], b.tfo[1].at[0], core).wait_recv()
    cp_o = pltpu.make_async_copy(b.fin[O].at[0], o_o, loc.at[3])
    cp_o.start()

    for cp in pending:
        cp.wait_send()
    for pred, cp in pending_if:
        pl.when(pred)(cp.wait_send)
    for u, r in ((1, 2), (0, 3)):
        rs_done(u, r)
    wo_drain()
    dwo_send(drain=True)

    @pl.when(mine)
    def _():
        for i, dev in enumerate(peers):
            rc(b.fin[O].at[0], b.fin[O].at[0], b.tfo[0].at[i], b.tfo[1].at[0], dev).wait_send()
    for cp in copies + [cp_out, cp_tg, cp_v, cp_o]:
        cp.wait()


def finish(divisor, q, *refs):
    ins, outs = refs[:7], refs[7:]
    for i in range(2):
        outs[i][...] = ins[i][...]
    for i in range(2, 6):
        outs[i][...] = ins[i][...].astype(F32) * (1.0 / divisor)

    @pl.when(pl.program_id(0) == 0)
    def _():
        v = ins[6][...] * (1.0 / divisor)
        for i in range(8):
            outs[6 + i][...] = v[i]
        for r in range(q.FF // q.D):
            outs[14][pl.ds(r * q.Dn, q.Dn)] = v[8 + r]


def body(n_dp, n_fsdp, tokens, patch_counts, gain_one, shift_one, joint_w, query_b, value_b, out_w,
         out_b, gain_two, shift_two, expand_w, expand_b, shrink_w, shrink_b, cotangent):
    R, D = tokens.shape
    q = Sizes(n_dp, n_fsdp, R, D, expand_w.shape[1], patch_counts.shape[1])
    q.grads = [(q.Z, q.Dn, 3 * q.DT), (q.ZT, q.Dn, D), (q.Z, q.Dn, q.F), (q.Z, q.FB, D)]
    scratch, tree = jax.tree.flatten(layout(q))
    anyspec = pl.BlockSpec(memory_space=pl.ANY)
    vmem = pl.BlockSpec(memory_space=pltpu.VMEM)
    sds = jax.ShapeDtypeStruct
    outs = pl.pallas_call(
        functools.partial(kernel, q, tree),
        out_shape=(
            sds((R, D), BF), sds((R, D), BF), sds((VROWS, q.Dn), F32),
            sds((q.Dn, 3 * D), BF), sds((q.Dn, D), BF), sds((q.Dn, q.FF), BF),
            sds((q.FF // q.n, D), BF)),
        in_specs=[anyspec, pl.BlockSpec(memory_space=pltpu.SMEM)] + [anyspec] * 5 + [vmem] * 9,
        out_specs=tuple([anyspec] * 7),
        scratch_shapes=scratch,
        compiler_params=pltpu.CompilerParams(
            collective_id=0, has_side_effects=True, vmem_limit_bytes=67043328),
        name="layer",
    )(tokens, patch_counts, joint_w, out_w, expand_w, shrink_w, cotangent,
      gain_one, shift_one, query_b, value_b, out_b, gain_two, shift_two, shrink_b, expand_b)
    result, tokens_grad, vec, gj, go_, ge, gs = outs
    divisor = float(n_dp * n_fsdp)
    mats = [gj, go_, ge, gs]
    if n_dp > q.T:
        groups = [[i + q.T * g for g in range(n_dp // q.T)] for i in range(q.T)]
        summed = lax.psum(tuple([vec] + mats), "dp", axis_index_groups=groups)
        vec, mats = summed[0], list(summed[1:])
    steps = 4
    blocked = lambda v: pl.BlockSpec((v.shape[0] // steps, v.shape[1]), lambda i: (i, 0))
    rows_in = [result, tokens_grad] + mats
    small = [q.Dn] * 8 + [q.FF // q.n]
    done = pl.pallas_call(
        functools.partial(finish, divisor, q),
        grid=(steps,),
        out_shape=tuple([sds(v.shape, BF) for v in rows_in[:2]] + [sds(v.shape, F32) for v in mats]
                        + [sds((k,), F32) for k in small]),
        in_specs=[blocked(v) for v in rows_in] + [vmem],
        out_specs=tuple([blocked(v) for v in rows_in] + [vmem] * 9),
        name="finish",
    )(*rows_in, vec)
    result, tokens_grad, gj, go_, ge, gs = done[:6]
    vec = done[6:]
    return (result, tokens_grad, vec[0], vec[1], gj, vec[2], vec[3], go_, vec[4], vec[5], vec[6],
            ge, vec[8], gs, vec[7])


def solution(mesh):
    rows = P(("dp", "fsdp"), None)
    vec, mat = P("fsdp"), P("fsdp", None)
    in_specs = (rows, rows, vec, vec, mat, vec, vec, mat, vec, vec, vec, mat, vec, mat, vec, rows)
    out_specs = (rows, rows, vec, vec, mat, vec, vec, mat, vec, vec, vec, mat, vec, mat, vec)
    fn = functools.partial(body, mesh.shape["dp"], mesh.shape["fsdp"])
    return jax.shard_map(fn, mesh=mesh, in_specs=in_specs, out_specs=out_specs, check_vma=False)
```

```python
import functools
from types import SimpleNamespace

import jax
import jax.numpy as jnp
from jax import lax
from jax.experimental import pallas as pl
from jax.experimental.pallas import tpu as pltpu
from jax.sharding import PartitionSpec as P

HEADS = 16
EPS = 1e-05
MASKED = -1e30
MESH = pl.DeviceIdType.MESH
BF = jnp.bfloat16
F32 = jnp.float32
VROWS = 16
J, O, E, S, VEC = range(5)


class Sizes:
    def __init__(self, n_dp, n_fsdp, rows, width, hidden, slots):
        self.n_dp, self.n = n_dp, n_fsdp
        self.R, self.D, self.FF, self.slots = rows, width, hidden, slots
        self.Y = 2 ** ((n_fsdp.bit_length() - 1) // 2)
        self.Z = n_fsdp // self.Y
        T = 4 if n_dp % 4 == 0 else 2
        while hidden // n_fsdp // T % 128 or self.Z % T:
            T //= 2
        self.T, self.X = T, T // 2
        self.RT = T * rows
        self.Dn = width // n_fsdp
        self.DT = width // T
        self.H = HEADS // T
        self.hd = width // HEADS
        self.F = hidden // T
        self.FB = hidden // n_fsdp // T
        self.ZT = self.Z // T
        self.OS = 2 if self.ZT <= 2 else 2 + self.ZT


def dot_nn(a, b):
    return jnp.dot(a, b, preferred_element_type=F32)


def dot_nt(a, b):
    return lax.dot_general(a, b, (((1,), (1,)), ((), ())), preferred_element_type=F32)


def dot_tn(a, b):
    return lax.dot_general(a, b, (((0,), (0,)), ((), ())), preferred_element_type=F32)


def ds(start, size, mult):
    return pl.ds(pl.multiple_of(start, mult), size)


def flip(v, k):
    r, bit = v, 1
    while bit <= k:
        if k & bit:
            r = r + bit - 2 * bit * (v // bit % 2)
        bit *= 2
    return r


def norm_parts(x):
    mean = jnp.mean(x, axis=-1, keepdims=True)
    xc = x - mean
    var = jnp.mean(xc * xc, axis=-1, keepdims=True)
    s = lax.rsqrt(var + EPS)
    return xc * s, s


def layout(q):
    R, D, T, RT = q.R, q.D, q.T, q.RT
    Cj = 3 * q.DT
    DMA = pltpu.SemaphoreType.DMA
    V = pltpu.VMEM
    m = SimpleNamespace()
    m.tok = V((T, R, D), BF)
    m.n1 = V((RT, D), BF)
    m.cot = V((T, R, D), BF)
    m.w = [V((D, Cj), BF), V((q.DT, D), BF), V((D, q.F), BF), V((q.F, D), BF)]
    m.qkv = V((RT, Cj), BF)
    m.prob = V((T * q.H, R, R), BF)
    m.mixed = V((RT, q.DT), BF)
    m.first = V((R, D), F32)
    m.n2 = V((T, R, D), BF)
    m.hact = V((RT, q.F), BF)
    m.dgelu = V((RT, q.F), BF)
    m.hgrad = V((RT, q.F), BF)
    m.proj = V((T, R, D), BF)
    m.fgrad = V((R, D), F32)
    m.mgrad = V((RT, q.DT), BF)
    m.jgrad = V((RT, Cj), BF)
    m.acc0 = V((R, D), F32)
    m.psend = [V((q.X, R, D), BF) for _ in range(2)]
    m.precv = [V((q.X, R, D), BF) for _ in range(2)]
    m.xsend = [V((R, D) if q.X == 2 else (16, 128), BF) for _ in range(2)]
    m.xrecv = [V((R, D) if q.X == 2 else (16, 128), BF) for _ in range(2)]
    m.rs = [[DMA((q.X,)), DMA((q.X,)), DMA((1,)), DMA((1,))] for _ in range(4)]
    m.dw = [V((bz, q.Y * rb, C), BF) for bz, rb, C in q.grads]
    m.yr = [V((q.Y - 1, bz, rb, C), BF) for bz, rb, C in q.grads]
    m.zr = [V((q.OS if w == O else q.Z - 1, rb, C), BF) for w, (bz, rb, C) in enumerate(q.grads)]
    m.zq = [V((16, 128) if w == O else (rb, C), BF) for w, (bz, rb, C) in enumerate(q.grads)]
    m.fin = [V((1 if w == O else T, rb, C), BF) for w, (bz, rb, C) in enumerate(q.grads)]
    m.sy = [[DMA((q.Y - 1, bz)), DMA((q.Y - 1, bz))] for bz, rb, C in q.grads]
    m.sz = [[DMA((max(q.Z - 1, q.ZT),)), DMA((max(q.Z, q.OS),))] for _ in q.grads]
    m.sout = [DMA((T, q.n)) for _ in q.grads]
    m.gz = [[DMA((q.Z,)), DMA((max(q.Z - 1, q.ZT),))] for _ in range(5)]
    m.gy = [[DMA((q.Y - 1, q.Z)), DMA((q.Y - 1, q.Z))] for _ in range(5)]
    pair = lambda: [DMA((3,)), DMA((3,))]
    m.ttok, m.tcot, m.tn2, m.tproj, m.tcnt, m.tfo = (pair() for _ in range(6))
    m.tfin = [pair() for _ in q.grads]
    m.vec = V((q.n, VROWS, q.Dn), BF)
    m.vf = V((8, D), F32)
    m.hb = V((8, q.F), F32)
    m.cnt = V((T, 8, 128), jnp.int32)
    m.vg = V((8, D), F32)
    m.vgh = V((8, q.F), F32)
    m.v3 = V((q.n, VROWS, q.Dn), F32)
    m.v3c = V((2, q.n, VROWS, q.Dn), F32)
    m.v3y = V((q.Y - 1, q.Z, VROWS, q.Dn), F32)
    m.v3s = V((q.Z, VROWS, q.Dn), F32)
    m.v3z = V((q.Z - 1, VROWS, q.Dn), F32)
    m.vout = V((VROWS, q.Dn), F32)
    m.svt = [DMA((2,)), DMA((2,))]
    m.svy = [DMA((q.Y - 1, q.Z)), DMA((q.Y - 1, q.Z))]
    m.svz = [DMA((q.Z - 1,)), DMA((q.Z - 1,))]
    m.loc = DMA((7 + q.n,))
    return vars(m)


def kernel(q, tree, *refs):
    (tokens, counts, joint_w, out_w, exp_w, shr_w, cotangent) = refs[:7]
    vectors = refs[7:16]
    (o_out, o_tg, o_vec, o_j, o_o, o_e, o_s) = refs[16:23]
    b = SimpleNamespace(**jax.tree.unflatten(tree, refs[23:]))
    R, D, T, X, RT, n, Y, Z = q.R, q.D, q.T, q.X, q.RT, q.n, q.Y, q.Z
    Dn, DT, F, FB, H, hd, ZT = q.Dn, q.DT, q.F, q.FB, q.H, q.hd, q.ZT
    Cj = 3 * DT

    dp = lax.axis_index("dp")
    s = lax.axis_index("fsdp")
    t = dp % T
    c, xx = t % 2, t // 2
    y, z = s % Y, s // Y
    core = (dp + 1 - 2 * c, s)
    xdp = dp + 2 - 4 * xx
    xpeer = (xdp, s)
    xcore = (xdp + 1 - 2 * c, s)
    tc = t + 1 - 2 * c
    if X == 2:
        tx = t + 2 - 4 * xx
        txc = tx + 1 - 2 * c
    zid = [flip(z, k) for k in range(Z)]
    relay = Z == 4
    inner = jnp.logical_and(z > 0, z < Z - 1)
    outer = jnp.logical_not(inner)
    zfar = jnp.where(z > 1, Z - 1, 0)
    yid = [(y + k) % Y for k in range(Y)]
    ysrc = [(y + Y - k) % Y for k in range(Y)]
    zpeer = [(dp, zid[k] * Y + y) for k in range(Z)]
    ypeer = [(dp, z * Y + yid[k]) for k in range(Y)]
    pending, pending_if = [], []

    def rc(src, dst, ss, rs, dev):
        return pltpu.make_async_remote_copy(
            src_ref=src, dst_ref=dst, send_sem=ss, recv_sem=rs,
            device_id=dev, device_id_type=MESH)

    def go(cp):
        cp.start()
        pending.append(cp)
        return cp

    def go_if(pred, cp):
        pl.when(pred)(cp.start)
        pending_if.append((pred, cp))

    loc = b.loc
    cp_tok = pltpu.make_async_copy(tokens, b.tok.at[t], loc.at[0])
    cp_cot = pltpu.make_async_copy(cotangent, b.cot.at[t], loc.at[1])
    cp_shr = pltpu.make_async_copy(
        shr_w.at[ds(t * FB, FB, 16)], b.w[S].at[ds(s * FB, FB, 16)], loc.at[3])
    cp_j = [pltpu.make_async_copy(
        joint_w.at[:, ds(j * D + t * DT, DT, 128)],
        b.w[J].at[ds(s * Dn, Dn, 16), pl.ds(j * DT, DT)], loc.at[4 + j]) for j in range(3)]
    cp_e = [pltpu.make_async_copy(
        exp_w.at[:, ds(i * (T * FB) + t * FB, FB, 128)],
        b.w[E].at[ds(s * Dn, Dn, 16), pl.ds(i * FB, FB)], loc.at[7 + i]) for i in range(n)]
    for cp in cp_j + [cp_tok] + cp_e + [cp_shr, cp_cot]:
        cp.start()

    lane = lax.broadcasted_iota(jnp.int32, (8, 128), 1)
    cv = jnp.zeros((8, 128), jnp.int32)
    for i in range(q.slots):
        cv = jnp.where(lane == i, counts[0, i], cv)
    b.cnt[t] = cv

    bar = pltpu.get_barrier_semaphore()
    greet = [core] + ([xpeer, xcore] if X == 2 else []) + zpeer[1:] + ypeer[1:]
    for dev in greet:
        pl.semaphore_signal(bar, inc=1, device_id=dev, device_id_type=MESH)
    pl.semaphore_wait(bar, len(greet))

    def slot(w, src_s):
        if w == VEC:
            return b.vec.at[src_s]
        if w == S:
            return b.w[S].at[ds(src_s * FB, FB, 16)]
        return b.w[w].at[ds(src_s * Dn, Dn, 16)]

    def gz_copy(w, k):
        return rc(slot(w, s), slot(w, s), b.gz[w][0].at[k - 1], b.gz[w][1].at[k - 1], zpeer[k])

    def gz_wait(w, k):
        src = slot(w, zid[k] * Y + y)
        rc(src, src, b.gz[w][0].at[k - 1], b.gz[w][1].at[k - 1], zpeer[k]).wait_recv()

    def gy_copies(w, k):
        src = slot(w, zid[k] * Y + y)
        return [rc(src, src, b.gy[w][0].at[m - 1, k], b.gy[w][1].at[m - 1, k], ypeer[m])
                for m in range(1, Y)]

    def ag_z(w):
        if not relay or w == VEC:
            for k in range(1, Z):
                go(gz_copy(w, k))
            return
        go(gz_copy(w, 1))
        go_if(inner, gz_copy(w, 3))
        go(gz_copy(w, 2))

    def ag_y(w, k):
        if k:
            gz_wait(w, k)
        if relay and w != VEC and k == 2:
            src = slot(w, zid[k] * Y + y)
            go_if(inner, rc(src, src, b.gz[w][0].at[Z - 1], b.gz[w][1].at[2], (dp, zfar * Y + y)))
        for cp in gy_copies(w, k):
            go(cp)

    def ag_y_if(pred, w, k):
        @pl.when(pred)
        def _():
            gz_wait(w, k)
            for cp in gy_copies(w, k):
                cp.start()

    def fw(w, *steps):
        for i in steps:
            if not relay or w == VEC:
                if i < Z:
                    ag_y(w, i)
            elif i == 2:
                ag_y_if(inner, w, 3)
            elif i == 4:
                ag_y_if(outer, w, 3)
                pending.extend(gy_copies(w, 3))
            else:
                ag_y(w, {0: 0, 1: 1, 3: 2}[i])

    def ag_wait(w):
        for k in range(Z):
            for m in range(1, Y):
                src = zid[k] * Y + ysrc[m]
                rc(slot(w, src), slot(w, src), b.gy[w][0].at[m - 1, k], b.gy[w][1].at[m - 1, k], ypeer[m]).wait_recv()

    zlo = t * ZT
    mine = z // ZT == t

    def wo_slot(zz, yy):
        return b.w[O].at[ds((zz * Y + yy) * Dn, Dn, 16)]

    def wo_z():
        @pl.when(mine)
        def _():
            zz = z - zlo
            for k in range(1, Z):
                rc(out_w, wo_slot(zz, y), b.gz[O][0].at[k - 1], b.gz[O][1].at[zz], zpeer[k]).start()
            pltpu.make_async_copy(out_w, wo_slot(zz, y), b.gz[O][1].at[zz]).start()

    def wo_y():
        for zz in range(ZT):
            pltpu.make_async_copy(out_w, wo_slot(zz, y), b.gz[O][1].at[zz]).wait()
            for m in range(1, Y):
                go(rc(wo_slot(zz, y), wo_slot(zz, y), b.gy[O][0].at[m - 1, zz], b.gy[O][1].at[m - 1, zz], ypeer[m]))

    def wo_wait():
        for zz in range(ZT):
            for m in range(1, Y):
                rc(wo_slot(zz, ysrc[m]), wo_slot(zz, ysrc[m]), b.gy[O][0].at[m - 1, zz], b.gy[O][1].at[m - 1, zz], ypeer[m]).wait_recv()

    def wo_drain():
        @pl.when(mine)
        def _():
            for k in range(1, Z):
                rc(out_w, wo_slot(z - zlo, y), b.gz[O][0].at[k - 1], b.gz[O][1].at[0], zpeer[k]).wait_send()

    def tp_send(buf, w, src=None):
        src = buf.at[t] if src is None else src
        if X == 2:
            go(rc(src, buf.at[t], w[0].at[1], w[1].at[1], xpeer))
        go(rc(src, buf.at[t], w[0].at[0], w[1].at[0], core))

    def tp_core(buf, w):
        rc(buf.at[tc], buf.at[tc], w[0].at[0], w[1].at[0], core).wait_recv()

    def tp_x(buf, w):
        if X == 2:
            rc(buf.at[tx], buf.at[tx], w[0].at[1], w[1].at[1], xpeer).wait_recv()
            go(rc(buf.at[tx], buf.at[tx], w[0].at[2], w[1].at[2], core))

    def tp_last(buf, w):
        if X == 2:
            rc(buf.at[txc], buf.at[txc], w[0].at[2], w[1].at[2], core).wait_recv()

    order = [(t, None), (tc, tp_core)] + ([(tx, tp_x), (txc, tp_last)] if X == 2 else [])

    vrow = lax.broadcasted_iota(jnp.int32, (VROWS, Dn), 0)
    packed = jnp.zeros((VROWS, Dn), F32)
    pieces = [v[...] for v in vectors[:8]]
    pieces += [vectors[8][pl.ds(r * Dn, Dn)] for r in range(vectors[8].shape[0] // Dn)]
    for i, piece in enumerate(pieces):
        packed = jnp.where(vrow == i, piece.astype(F32).reshape(1, Dn), packed)
    b.vec[s] = packed.astype(BF)
    ag_z(VEC)
    ag_y(VEC, 0)
    cnt = b.cnt
    peers = [core] + ([xpeer, xcore] if X == 2 else [])
    for i, dev in enumerate(peers):
        go(rc(cnt.at[t], cnt.at[t], b.tcnt[0].at[i], b.tcnt[1].at[i], dev))
    for cp in cp_j:
        cp.wait()
    ag_z(J)
    fw(J, 0)
    cp_tok.wait()
    tp_send(b.tok, b.ttok)
    last = range(4, max(Z, 5))

    fw(VEC, *range(1, Z))
    for cp in cp_e:
        cp.wait()
    fw(E, 0)
    ag_wait(VEC)
    vf, hb = b.vf, b.hb
    for i in range(n):
        piece = b.vec[i].astype(F32)
        vf[:, i * Dn:(i + 1) * Dn] = piece[0:8]
        kk = FB // Dn
        for r in range(kk):
            row = piece[8 + r:9 + r]
            for g in range(1, T):
                row = jnp.where(t == g, piece[8 + g * kk + r:9 + g * kk + r], row)
            hb[0:1, i * FB + r * Dn:i * FB + (r + 1) * Dn] = row
    vg, vgh = b.vg, b.vgh
    vg[...] = jnp.zeros_like(vg)

    for i, st in enumerate([tc] + ([tx, txc] if X == 2 else [])):
        rc(cnt.at[st], cnt.at[st], b.tcnt[0].at[i], b.tcnt[1].at[i], peers[i]).wait_recv()

    def ends_of(g):
        row = cnt[g]
        ends, total = [], None
        for i in range(q.slots):
            v = row[0:1, i:i + 1]
            total = v if total is None else total + v
            ends.append(total)
        return ends

    RB = 64
    nrb = R // RB

    def live_of(ends, r0, rows):
        places = lax.broadcasted_iota(jnp.int32, (rows, 1), 0) + r0
        return (places < ends[-1]).astype(F32)

    fw(J, 1)
    own_ends = ends_of(t)
    cp_cot.wait()
    cot = b.cot

    def cot_step(i, acc):
        r0 = pl.multiple_of(i * RB, RB)
        v = cot[t, pl.ds(r0, RB), :].astype(F32) * live_of(own_ends, r0, RB)
        cot[t, pl.ds(r0, RB), :] = v.astype(BF)
        return acc + jnp.sum(v, axis=0, keepdims=True)

    vg[7:8, :] = lax.fori_loop(0, nrb, cot_step, jnp.zeros((1, D), F32))
    tp_send(cot, b.tcot)

    tok, n1 = b.tok, b.n1

    def ln1(g):
        def step(i, _):
            r0 = pl.multiple_of(i * RB, RB)
            nn, _s = norm_parts(tok[g, pl.ds(r0, RB), :].astype(F32))
            n1[ds(g * R + r0, RB, RB), :] = (nn * vf[0:1, :] + vf[1:2, :]).astype(BF)
            return 0
        lax.fori_loop(0, nrb, step, 0)

    ln1(t)
    fw(J, 2)
    tp_core(tok, b.ttok)
    ln1(tc)
    wo_z()
    fw(J, 3)
    tp_x(tok, b.ttok)
    if X == 2:
        ln1(tx)
    fw(J, *last)
    if X == 2:
        tp_last(tok, b.ttok)
        ln1(txc)
    ag_wait(J)
    ag_z(E)
    qkv, wj = b.qkv, b.w[J]
    TN = 256
    for j in range(3):
        def step(i, _, j=j):
            col = j * DT + i * TN
            r = dot_nn(n1[...], wj[:, ds(col, TN, 128)])
            if j != 1:
                r = r + vf[(2 if j == 0 else 3):(3 if j == 0 else 4), ds(t * DT + i * TN, TN, 128)]
            qkv[:, ds(col, TN, 128)] = r.astype(BF)
            return 0
        lax.fori_loop(0, DT // TN, step, 0)

    wo_y()
    scale = hd ** (-0.5)
    prob, mixed = b.prob, b.mixed
    AW = 256
    GH = AW // hd
    lanes = lax.broadcasted_iota(jnp.int32, (1, AW), 1)
    head_masks = [(lanes // hd == h) for h in range(GH)]

    def hm(v, h):
        return jnp.where(head_masks[h], v, jnp.zeros_like(v))

    def attend(g):
        ends = ends_of(g)
        ri = lax.broadcasted_iota(jnp.int32, (R, R), 0)
        ci = lax.broadcasted_iota(jnp.int32, (R, R), 1)
        im_r = jnp.zeros((R, R), jnp.int32)
        im_c = jnp.zeros((R, R), jnp.int32)
        for e in ends:
            im_r = im_r + (ri >= e).astype(jnp.int32)
            im_c = im_c + (ci >= e).astype(jnp.int32)
        same = im_r == im_c
        rows = ds(g * R, R, 256)
        for a in range(DT // AW):
            qa = qkv[rows, pl.ds(a * AW, AW)]
            ka = qkv[rows, pl.ds(DT + a * AW, AW)]
            va = qkv[rows, pl.ds(2 * DT + a * AW, AW)]
            acc = None
            for h in range(GH):
                sc = dot_nt(hm(qa, h), ka) * scale
                sc = jnp.where(same, sc, MASKED)
                top = jnp.max(sc, axis=-1, keepdims=True)
                ex = jnp.exp(sc - top)
                tot = jnp.sum(ex, axis=-1, keepdims=True)
                p = (ex * (1.0 / tot)).astype(BF)
                prob[g * H + a * GH + h] = p
                part = dot_nn(p, hm(va, h))
                acc = part if acc is None else acc + part
            mixed[rows, pl.ds(a * AW, AW)] = acc.astype(BF)

    def att_step(g, _):
        attend(g)
        return 0

    lax.fori_loop(0, T, att_step, 0)
    cp_shr.wait()
    ag_z(S)
    fw(E, 1)
    wo_wait()

    acc0 = b.acc0

    def block_mm(lhs, g, rhs, nt, put):
        def step(i, _):
            cols = ds(i * TN, TN, 256)
            a = lhs[ds(g * R, R, 256), :]
            put(cols, dot_nt(a, rhs[cols, :]) if nt else dot_nn(a, rhs[:, cols]))
            return 0
        lax.fori_loop(0, D // TN, step, 0)

    def rs_copy(u, r, i):
        return rc(b.psend[u].at[i], b.precv[u].at[i], b.rs[r][0].at[i], b.rs[r][1].at[i], core)

    def rs_xcopy(u, r):
        return rc(b.xsend[u], b.xrecv[u], b.rs[r][2].at[0], b.rs[r][3].at[0], xpeer)

    def rs_start(u, r, lhs, rhs, nt, put_own=None):
        ps = b.psend[u]

        def put_at(i):
            def put(cols, v):
                ps[i, :, cols] = v.astype(BF)
            return put

        def put_acc(cols, v):
            acc0[:, cols] = v

        if X == 2:
            block_mm(lhs, txc, rhs, nt, put_at(1))
            rs_copy(u, r, 1).start()
            block_mm(lhs, tx, rhs, nt, put_acc)
            rs_copy(u, r, 1).wait_recv()
            pr, xs = b.precv[u], b.xsend[u]

            def add(i, _):
                rows = ds(i * RB, RB, RB)
                xs[rows, :] = (acc0[rows, :] + pr[1, rows, :].astype(F32)).astype(BF)
                return 0
            lax.fori_loop(0, nrb, add, 0)
            rs_xcopy(u, r).start()
        block_mm(lhs, tc, rhs, nt, put_at(0))
        rs_copy(u, r, 0).start()
        block_mm(lhs, t, rhs, nt, put_own or put_acc)

    def rs_wait(u, r):
        rs_copy(u, r, 0).wait_recv()
        if X == 2:
            rs_xcopy(u, r).wait_recv()

    def rs_value(u, rows, own=True):
        v = b.precv[u][0, rows, :].astype(F32)
        if own:
            v = acc0[rows, :] + v
        if X == 2:
            v = v + b.xrecv[u][rows, :].astype(F32)
        return v

    def rs_done(u, r):
        for i in range(X):
            rs_copy(u, r, i).wait_send()
        if X == 2:
            rs_xcopy(u, r).wait_send()

    rs_start(0, 0, mixed, b.w[O], False)
    tp_core(cot, b.tcot)
    tp_x(cot, b.tcot)
    fw(E, 2)
    fw(E, 3)
    fw(S, 0)
    fw(E, *last)
    rs_wait(0, 0)
    first, n2 = b.first, b.n2

    def ln2(i, _):
        rows = ds(i * RB, RB, RB)
        v = tok[t, rows, :].astype(F32) + (rs_value(0, rows) + vf[4:5, :])
        first[rows, :] = v
        nn, _s = norm_parts(v)
        n2[t, rows, :] = (nn * vf[5:6, :] + vf[6:7, :]).astype(BF)
        return 0
    lax.fori_loop(0, nrb, ln2, 0)
    tp_send(n2, b.tn2)
    rs_done(0, 0)
    tp_last(cot, b.tcot)
    fw(S, 1)
    ag_wait(E)

    hact, dgelu, we, ws = b.hact, b.dgelu, b.w[E], b.w[S]

    def up(g):
        def step(i, _):
            cols = ds(i * TN, TN, 256)
            rows = ds(g * R, R, 256)
            h = dot_nn(n2[g], we[:, cols]) + hb[0:1, cols]
            phi = 0.5 * (1.0 + lax.erf(h * 0.7071067811865476))
            hact[rows, cols] = (h * phi).astype(BF)
            dgelu[rows, cols] = (phi + h * (jnp.exp(-0.5 * h * h) * 0.3989422804014327)).astype(BF)
            return 0
        lax.fori_loop(0, F // TN, step, 0)

    up(t)
    tp_core(n2, b.tn2)
    up(tc)
    fw(S, 2)
    fw(S, 3)
    tp_x(n2, b.tn2)
    if X == 2:
        up(tx)
        tp_last(n2, b.tn2)
        up(txc)
    fw(S, *last)

    def blocks(w):
        return q.grads[w]

    def dw_dest(w, k):
        return zlo + k if w == O else zid[k]

    def dw_slot(w, k):
        return k if w == O else zid[k]

    def dw_y(w, sl, m):
        rb = blocks(w)[1]
        return rc(b.dw[w].at[sl, ds(yid[m] * rb, rb, 16)], b.yr[w].at[m - 1, sl],
                  b.sy[w][0].at[m - 1, sl], b.sy[w][1].at[m - 1, sl], ypeer[m])

    def dw_compute(w, k, lhs, rhs):
        bz, rb, C = blocks(w)
        sl = dw_slot(w, k)
        tile = Y * rb
        TC = 256

        def step(i, _):
            cols = ds(i * TC, TC, 256)
            for r in range(tile // 256):
                a = lhs(sl * tile + r * 256)
                b.dw[w][sl, pl.ds(r * 256, 256), cols] = dot_tn(a, rhs(cols)).astype(BF)
            return 0
        lax.fori_loop(0, C // TC, step, 0)
        for m in range(1, Y):
            go(dw_y(w, sl, m))

    def dw_sum(w, k):
        bz, rb, C = blocks(w)
        sl = dw_slot(w, k)
        for m in range(1, Y):
            dw_y(w, sl, m).wait_recv()
        ch = 64

        def add(i, _):
            rows = ds(y * rb + i * ch, ch, 64)
            v = b.dw[w][sl, rows, :].astype(F32)
            for m in range(1, Y):
                v = v + b.yr[w][m - 1, sl, ds(i * ch, ch, 64), :].astype(F32)
            b.dw[w][sl, rows, :] = v.astype(BF)
            return 0
        lax.fori_loop(0, rb // ch, add, 0)

    def dw_z(w, k):
        rb = blocks(w)[1]
        return rc(b.dw[w].at[zid[k], ds(y * rb, rb, 16)], b.zr[w].at[k - 1],
                  b.sz[w][0].at[k - 1], b.sz[w][1].at[k - 1], zpeer[k])

    def dw_o(zz, i, to):
        return rc(b.dw[O].at[zz, ds(y * Dn, Dn, 16)], b.zr[O].at[i], b.sz[O][0].at[zz],
                  b.sz[O][1].at[i], (dp, to * Y + y))

    def relay_slot(zz):
        return zz if ZT <= 2 else 2 + zz

    def dw_relay(w):
        rb = blocks(w)[1]
        return rc(b.dw[w].at[zid[3], ds(y * rb, rb, 16)], b.zq[w], b.sz[w][0].at[2],
                  b.sz[w][1].at[Z - 1], zpeer[1])

    def dw_send(w, k):
        dw_sum(w, k)
        if relay and k == 3:
            go_if(inner, dw_z(w, k))
            go_if(outer, dw_relay(w))
            return
        if relay and k == 2:
            @pl.when(inner)
            def _():
                dw_relay(w).wait_recv()
                rb, ch = blocks(w)[1], 64

                def add(i, _):
                    rows = ds(y * rb + i * ch, ch, 64)
                    v = b.dw[w][zid[2], rows, :].astype(F32) + b.zq[w][ds(i * ch, ch, 64), :].astype(F32)
                    b.dw[w][zid[2], rows, :] = v.astype(BF)
                    return 0
                lax.fori_loop(0, rb // ch, add, 0)
        if k:
            go(dw_z(w, k))

    def dwo_hops(act_near, act_far):
        for zz in range(ZT):
            zo = zlo + zz
            far = z // 2 != zo // 2
            near = jnp.logical_and(z // 2 == zo // 2, z != zo)
            if Z > 1:
                pl.when(near)(lambda zz=zz, zo=zo: act_near(dw_o(zz, 0, zo)))
            if Z > 2:
                pl.when(jnp.logical_and(far, outer))(lambda zz=zz: act_near(dw_o(zz, relay_slot(zz), zid[1])))
                pl.when(jnp.logical_and(far, inner))(lambda zz=zz, zo=zo: act_far(zz, dw_o(zz, 1, zo)))

    def dwo_first():
        for zz in range(ZT):
            dw_sum(O, zz)
        dwo_hops(lambda cp: cp.start(), lambda zz, cp: None)

    def dwo_second():
        def pass_on(zz, cp):
            dw_o(zz, relay_slot(zz), z).wait_recv()
            ch = 64

            def add(j, _):
                rows = ds(y * Dn + j * ch, ch, 64)
                v = b.dw[O][zz, rows, :].astype(F32) + b.zr[O][relay_slot(zz), ds(j * ch, ch, 64), :].astype(F32)
                b.dw[O][zz, rows, :] = v.astype(BF)
                return 0
            lax.fori_loop(0, Dn // ch, add, 0)
            cp.start()
        dwo_hops(lambda cp: None, pass_on)

    def dw_final(w):
        bz, rb, C = blocks(w)
        ch = 64
        fin = b.fin[w]
        own = z - zlo if w == O else z
        me = 0 if w == O else t

        def total(slots):
            def add(i, _):
                rows = ds(i * ch, ch, 64)
                v = b.dw[w][own, ds(y * rb + i * ch, ch, 64), :].astype(F32)
                for i_slot in slots:
                    v = v + b.zr[w][i_slot, rows, :].astype(F32)
                fin[me, rows, :] = v.astype(BF)
                return 0
            lax.fori_loop(0, rb // ch, add, 0)

        def wait_total(ks):
            for k in ks:
                dw_z(w, k).wait_recv()
            total([k - 1 for k in ks])

        if w == O:
            ends = range(min(Z - 1, 2))
            for i in ends:
                dw_o(own, i, z).wait_recv()
            total(ends)
        elif relay:
            pl.when(inner)(lambda: wait_total((1, 2, 3)))
            pl.when(outer)(lambda: wait_total((1, 2)))
        else:
            wait_total(range(1, Z))
        if w != O:
            tp_send(fin, b.tfin[w])

    def out_copies(w, g):
        fin, so = b.fin[w], b.sout[w]
        if w == J:
            return [pltpu.make_async_copy(fin.at[g, :, pl.ds(j * DT, DT)],
                    o_j.at[:, ds(j * D + g * DT, DT, 128)], so.at[g, j]) for j in range(3)]
        if w == E:
            return [pltpu.make_async_copy(fin.at[g, :, pl.ds(i * FB, FB)],
                    o_e.at[:, ds(i * (T * FB) + g * FB, FB, 128)], so.at[g, i]) for i in range(n)]
        return [pltpu.make_async_copy(fin.at[g], o_s.at[ds(g * FB, FB, 16)], so.at[g, 0])]

    def cot_rhs(cols):
        return cot[:, :, cols].reshape(RT, 256)

    zorder = ([3, 2, 1] if relay else list(range(1, Z))) + [0]
    half = len(zorder) // 2

    def dw_shrink(ks):
        for k in ks:
            dw_compute(S, k, lambda c0: hact[:, ds(c0, 256, 256)], cot_rhs)

    dw_shrink(zorder[:half])
    dw_shrink(zorder[half:])
    ag_wait(S)
    hgrad = b.hgrad

    def down(g, acc):
        def step(i, _):
            cols = ds(i * TN, TN, 256)
            rows = ds(g * R, R, 256)
            v = dot_nt(cot[g], ws[cols, :]) * dgelu[rows, cols].astype(F32)
            hgrad[rows, cols] = v.astype(BF)
            return 0
        lax.fori_loop(0, F // TN, step, 0)
        return acc

    lax.fori_loop(0, T, down, 0)
    def send(w, *steps):
        for i in steps:
            if i < Z:
                dw_send(w, zorder[i])

    send(S, 0)
    rs_start(0, 1, hgrad, we, True)
    send(S, 1)

    def dw_expand(ks):
        for k in ks:
            dw_compute(E, k, lambda c0: n2[:, :, ds(c0, 256, 256)].reshape(RT, 256),
                       lambda cols: hgrad[:, cols])

    dw_expand(zorder[:half])
    send(S, 2)
    dw_expand(zorder[half:])
    rs_wait(0, 1)
    proj, fgrad = b.proj, b.fgrad

    def ln2_back(i, carry):
        ag_, as_, ab_ = carry
        rows = ds(i * RB, RB, RB)
        two = rs_value(0, rows)
        nn, sd = norm_parts(first[rows, :])
        e = two * vf[5:6, :]
        og = cot[t, rows, :].astype(F32)
        fg = og + sd * (e - jnp.mean(e, axis=-1, keepdims=True)
                        - nn * jnp.mean(e * nn, axis=-1, keepdims=True))
        fgrad[rows, :] = fg
        pj = fg.astype(BF)
        proj[t, rows, :] = pj
        return (ag_ + jnp.sum(two * nn, axis=0, keepdims=True),
                as_ + jnp.sum(two, axis=0, keepdims=True),
                ab_ + jnp.sum(pj.astype(F32), axis=0, keepdims=True))

    zrow = jnp.zeros((1, D), F32)
    g2, s2, ob = lax.fori_loop(0, nrb, ln2_back, (zrow, zrow, zrow))
    tp_send(proj, b.tproj)
    vg[5:6, :] = g2
    vg[6:7, :] = s2
    vg[4:5, :] = ob
    rs_done(0, 1)

    send(S, *range(3, Z))
    def add_to_first(cols, v):
        first[:, cols] = first[:, cols] + v

    rs_start(1, 2, hact, ws, False, add_to_first)

    def hb_step(i, _):
        cols = ds(i * TN, TN, 256)
        vgh[0:1, cols] = jnp.sum(hgrad[:, cols].astype(F32), axis=0, keepdims=True)
        return 0
    lax.fori_loop(0, F // TN, hb_step, 0)
    mgrad, jgrad, wo = b.mgrad, b.jgrad, b.w[O]

    def mixed_back(g):
        def step(i, _):
            cols = ds(i * TN, TN, 256)
            mgrad[ds(g * R, R, 256), cols] = dot_nt(proj[g], wo[cols, :]).astype(BF)
            return 0
        lax.fori_loop(0, DT // TN, step, 0)

    def attend_back(g):
        rows = ds(g * R, R, 256)
        for a in range(DT // AW):
            qa = qkv[rows, pl.ds(a * AW, AW)]
            ka = qkv[rows, pl.ds(DT + a * AW, AW)]
            va = qkv[rows, pl.ds(2 * DT + a * AW, AW)]
            ma = mgrad[rows, pl.ds(a * AW, AW)]
            aq = ak = av = None
            for h in range(GH):
                mh = hm(ma, h)
                pg = dot_nt(mh, va)
                pl_ = prob[g * H + a * GH + h]
                p = pl_.astype(F32)
                inner = jnp.sum(p * pg, axis=-1, keepdims=True)
                sg = (p * (pg - inner)).astype(BF)
                dq = dot_nn(sg, hm(ka, h))
                dk = dot_tn(sg, hm(qa, h))
                dv = dot_tn(pl_, mh)
                aq = dq if aq is None else aq + dq
                ak = dk if ak is None else ak + dk
                av = dv if av is None else av + dv
            jgrad[rows, pl.ds(a * AW, AW)] = (aq * scale).astype(BF)
            jgrad[rows, pl.ds(DT + a * AW, AW)] = (ak * scale).astype(BF)
            jgrad[rows, pl.ds(2 * DT + a * AW, AW)] = av.astype(BF)

    obuf = n2.at[tc]

    def out_step(i, _):
        rows = ds(i * RB, RB, RB)
        r0 = i * RB
        v = (first[rows, :] + rs_value(1, rows, False) + vf[7:8, :]) * live_of(own_ends, r0, RB)
        obuf[rows, :] = v.astype(BF)
        return 0
    def attb_step(g, _):
        attend_back(g)
        return 0

    send(E, 0)
    mixed_back(t)
    tp_core(proj, b.tproj)
    mixed_back(tc)
    attend_back(t)
    tp_x(proj, b.tproj)
    attend_back(tc)
    if X == 2:
        mixed_back(tx)
        attend_back(tx)
    send(E, 1)
    tp_last(proj, b.tproj)
    dw_final(S)
    for zz in range(ZT):
        dw_compute(O, zz, lambda c0: mixed[:, ds(c0, 256, 256)],
                   lambda cols: proj[:, :, cols].reshape(RT, 256))
    if X == 2:
        mixed_back(txc)
        attend_back(txc)
    send(E, 2)
    rs_start(0, 3, jgrad, wj, True)
    for k in zorder:
        dw_compute(J, k, lambda c0: n1[:, ds(c0, 256, 256)], lambda cols: jgrad[:, cols])
    dwo_first()
    send(E, *range(3, Z))
    dw_final(E)
    rs_wait(1, 2)
    lax.fori_loop(0, nrb, out_step, 0)
    cp_out = pltpu.make_async_copy(obuf, o_out, loc.at[0])
    cp_out.start()
    for i in range(2):
        j = 2 * i
        vg[2 + i:3 + i, ds(t * DT, DT, 128)] = jnp.sum(
            jgrad[:, pl.ds(j * DT, DT)].astype(F32), axis=0, keepdims=True)
    send(J, 0)
    dwo_second()
    send(J, 1)
    send(J, 2)
    rs_wait(0, 3)
    tbuf = proj.at[tc]

    def ln1_back(i, carry):
        ag_, as_ = carry
        rows = ds(i * RB, RB, RB)
        one = rs_value(0, rows)
        nn, sd = norm_parts(tok[t, rows, :].astype(F32))
        e = one * vf[0:1, :]
        v = fgrad[rows, :] + sd * (e - jnp.mean(e, axis=-1, keepdims=True)
                                   - nn * jnp.mean(e * nn, axis=-1, keepdims=True))
        tbuf[rows, :] = v.astype(BF)
        return (ag_ + jnp.sum(one * nn, axis=0, keepdims=True),
                as_ + jnp.sum(one, axis=0, keepdims=True))

    g1, s1 = lax.fori_loop(0, nrb, ln1_back, (zrow, zrow))
    cp_tg = pltpu.make_async_copy(tbuf, o_tg, loc.at[1])
    cp_tg.start()
    vg[0:1, :] = g1
    vg[1:2, :] = s1

    v3, v3c = b.v3, b.v3c
    kk = FB // Dn
    v3[...] = jnp.zeros_like(v3)
    for i in range(n):
        v3[i, 0:8, :] = vg[:, i * Dn:(i + 1) * Dn]
        for r in range(kk):
            row = vgh[0:1, i * FB + r * Dn:i * FB + (r + 1) * Dn]
            for g in range(T):
                v3[i, 8 + g * kk + r:9 + g * kk + r, :] = jnp.where(t == g, row, jnp.zeros_like(row))
    vt = rc(v3, v3c.at[0], b.svt[0].at[0], b.svt[1].at[0], core)
    vt.start()
    send(J, *range(3, Z))
    vt.wait()
    v3[...] = v3[...] + v3c[0]
    if X == 2:
        vx = rc(v3, v3c.at[1], b.svt[0].at[1], b.svt[1].at[1], xpeer)
        vx.start()
    owner = z // ZT

    def fo_copy(i, dev):
        return rc(b.fin[O].at[0], b.fin[O].at[0], b.tfo[0].at[i], b.tfo[1].at[0], dev)

    @pl.when(mine)
    def _():
        dw_final(O)
        fo_copy(0, core).start()
        if X == 2:
            fo_copy(1, xpeer).start()
    if X == 2:
        vx.wait()
        v3[...] = v3[...] + v3c[1]
    v3y, v3s, v3z = b.v3y, b.v3s, b.v3z

    def vy(m, k):
        return rc(v3.at[zid[k] * Y + yid[m]], v3y.at[m - 1, zid[k]], b.svy[0].at[m - 1, zid[k]],
                  b.svy[1].at[m - 1, zid[k]], ypeer[m])
    for k in range(Z):
        for m in range(1, Y):
            go(vy(m, k))

    copies = []

    def emit(w, g):
        for cp in out_copies(w, g):
            cp.start()
            copies.append(cp)

    emit(S, t)
    tp_core(b.fin[S], b.tfin[S])
    emit(S, tc)
    tp_x(b.fin[S], b.tfin[S])
    if X == 2:
        emit(S, tx)
    dw_final(J)

    def vz(k):
        return rc(v3s.at[k], v3z.at[k - 1], b.svz[0].at[k - 1], b.svz[1].at[k - 1], zpeer[k])
    for k in zorder:
        v = v3[zid[k] * Y + y]
        for m in range(1, Y):
            vy(m, k).wait_recv()
            v = v + v3y[m - 1, zid[k]]
        v3s[k] = v
        if k:
            go(vz(k))

    @pl.when(jnp.logical_not(mine))
    def _():
        fo_copy(0, core).wait_recv()
    if X == 2:
        pl.when(tx == owner)(lambda: fo_copy(2, core).start())
    cp_o = pltpu.make_async_copy(b.fin[O].at[0], o_o, loc.at[3])
    cp_o.start()
    emit(E, t)
    tp_core(b.fin[E], b.tfin[E])
    emit(E, tc)
    tp_x(b.fin[E], b.tfin[E])
    if X == 2:
        emit(E, tx)

    v = v3s[0]
    for k in range(1, Z):
        vz(k).wait_recv()
        v = v + v3z[k - 1]
    b.vout[...] = v
    cp_v = pltpu.make_async_copy(b.vout, o_vec, loc.at[2])
    cp_v.start()

    emit(J, t)
    tp_core(b.fin[J], b.tfin[J])
    emit(J, tc)
    tp_x(b.fin[J], b.tfin[J])
    for w in (S, E, J):
        tp_last(b.fin[w], b.tfin[w])
        if X == 2:
            emit(w, txc)
    if X == 2:
        emit(J, tx)

    for cp in pending:
        cp.wait_send()
    for pred, cp in pending_if:
        pl.when(pred)(cp.wait_send)
    for u, r in ((1, 2), (0, 3)):
        rs_done(u, r)
    wo_drain()
    dwo_hops(lambda cp: cp.wait_send(), lambda zz, cp: cp.wait_send())

    @pl.when(mine)
    def _():
        fo_copy(0, core).wait_send()
        if X == 2:
            fo_copy(1, xpeer).wait_send()
    if X == 2:
        pl.when(tx == owner)(lambda: fo_copy(2, core).wait_send())
    for cp in copies + [cp_out, cp_tg, cp_v, cp_o]:
        cp.wait()


def finish(divisor, q, *refs):
    ins, outs = refs[:7], refs[7:]
    for i in range(2):
        outs[i][...] = ins[i][...]
    for i in range(2, 6):
        outs[i][...] = ins[i][...].astype(F32) * (1.0 / divisor)

    @pl.when(pl.program_id(0) == 0)
    def _():
        v = ins[6][...] * (1.0 / divisor)
        for i in range(8):
            outs[6 + i][...] = v[i]
        for r in range(q.FF // q.D):
            outs[14][pl.ds(r * q.Dn, q.Dn)] = v[8 + r]


def body(n_dp, n_fsdp, tokens, patch_counts, gain_one, shift_one, joint_w, query_b, value_b, out_w,
         out_b, gain_two, shift_two, expand_w, expand_b, shrink_w, shrink_b, cotangent):
    R, D = tokens.shape
    q = Sizes(n_dp, n_fsdp, R, D, expand_w.shape[1], patch_counts.shape[1])
    q.grads = [(q.Z, q.Dn, 3 * q.DT), (q.ZT, q.Dn, D), (q.Z, q.Dn, q.F), (q.Z, q.FB, D)]
    scratch, tree = jax.tree.flatten(layout(q))
    anyspec = pl.BlockSpec(memory_space=pl.ANY)
    vmem = pl.BlockSpec(memory_space=pltpu.VMEM)
    sds = jax.ShapeDtypeStruct
    outs = pl.pallas_call(
        functools.partial(kernel, q, tree),
        out_shape=(
            sds((R, D), BF), sds((R, D), BF), sds((VROWS, q.Dn), F32),
            sds((q.Dn, 3 * D), BF), sds((q.Dn, D), BF), sds((q.Dn, q.FF), BF),
            sds((q.FF // q.n, D), BF)),
        in_specs=[anyspec, pl.BlockSpec(memory_space=pltpu.SMEM)] + [anyspec] * 5 + [vmem] * 9,
        out_specs=tuple([anyspec] * 7),
        scratch_shapes=scratch,
        compiler_params=pltpu.CompilerParams(
            collective_id=0, has_side_effects=True, vmem_limit_bytes=67043328),
        name="layer",
    )(tokens, patch_counts, joint_w, out_w, expand_w, shrink_w, cotangent,
      gain_one, shift_one, query_b, value_b, out_b, gain_two, shift_two, shrink_b, expand_b)
    result, tokens_grad, vec, gj, go_, ge, gs = outs
    divisor = float(n_dp * n_fsdp)
    mats = [gj, go_, ge, gs]
    if n_dp > q.T:
        groups = [[i + q.T * g for g in range(n_dp // q.T)] for i in range(q.T)]
        summed = lax.psum(tuple([vec] + mats), "dp", axis_index_groups=groups)
        vec, mats = summed[0], list(summed[1:])
    steps = 4
    blocked = lambda v: pl.BlockSpec((v.shape[0] // steps, v.shape[1]), lambda i: (i, 0))
    rows_in = [result, tokens_grad] + mats
    small = [q.Dn] * 8 + [q.FF // q.n]
    done = pl.pallas_call(
        functools.partial(finish, divisor, q),
        grid=(steps,),
        out_shape=tuple([sds(v.shape, BF) for v in rows_in[:2]] + [sds(v.shape, F32) for v in mats]
                        + [sds((k,), F32) for k in small]),
        in_specs=[blocked(v) for v in rows_in] + [vmem],
        out_specs=tuple([blocked(v) for v in rows_in] + [vmem] * 9),
        name="finish",
    )(*rows_in, vec)
    result, tokens_grad, gj, go_, ge, gs = done[:6]
    vec = done[6:]
    return (result, tokens_grad, vec[0], vec[1], gj, vec[2], vec[3], go_, vec[4], vec[5], vec[6],
            ge, vec[8], gs, vec[7])


def solution(mesh):
    rows = P(("dp", "fsdp"), None)
    vec, mat = P("fsdp"), P("fsdp", None)
    in_specs = (rows, rows, vec, vec, mat, vec, vec, mat, vec, vec, vec, mat, vec, mat, vec, rows)
    out_specs = (rows, rows, vec, vec, mat, vec, vec, mat, vec, vec, vec, mat, vec, mat, vec)
    fn = functools.partial(body, mesh.shape["dp"], mesh.shape["fsdp"])
    return jax.shard_map(fn, mesh=mesh, in_specs=in_specs, out_specs=out_specs, check_vma=False)
```

```python
import functools
from types import SimpleNamespace

import jax
import jax.numpy as jnp
from jax import lax
from jax.experimental import pallas as pl
from jax.experimental.pallas import tpu as pltpu
from jax.sharding import PartitionSpec as P

HEADS = 16
EPS = 1e-05
MASKED = -1e30
MESH = pl.DeviceIdType.MESH
BF = jnp.bfloat16
F32 = jnp.float32
VROWS = 16
J, O, E, S, VEC = range(5)


class Sizes:
    def __init__(self, n_dp, n_fsdp, rows, width, hidden, slots):
        self.n_dp, self.n = n_dp, n_fsdp
        self.R, self.D, self.FF, self.slots = rows, width, hidden, slots
        self.Y = 2 ** ((n_fsdp.bit_length() - 1) // 2)
        self.Z = n_fsdp // self.Y
        T = 4 if n_dp % 4 == 0 else 2
        while hidden // n_fsdp // T % 128 or self.Z % T:
            T //= 2
        self.T, self.X = T, T // 2
        self.RT = T * rows
        self.Dn = width // n_fsdp
        self.DT = width // T
        self.H = HEADS // T
        self.hd = width // HEADS
        self.F = hidden // T
        self.FB = hidden // n_fsdp // T
        self.ZT = self.Z // T
        self.OS = 2 if self.ZT <= 2 else 2 + self.ZT


def dot_nn(a, b):
    return jnp.dot(a, b, preferred_element_type=F32)


def dot_nt(a, b):
    return lax.dot_general(a, b, (((1,), (1,)), ((), ())), preferred_element_type=F32)


def dot_tn(a, b):
    return lax.dot_general(a, b, (((0,), (0,)), ((), ())), preferred_element_type=F32)


def ds(start, size, mult):
    return pl.ds(pl.multiple_of(start, mult), size)


def flip(v, k):
    r, bit = v, 1
    while bit <= k:
        if k & bit:
            r = r + bit - 2 * bit * (v // bit % 2)
        bit *= 2
    return r


def norm_parts(x):
    mean = jnp.mean(x, axis=-1, keepdims=True)
    xc = x - mean
    var = jnp.mean(xc * xc, axis=-1, keepdims=True)
    s = lax.rsqrt(var + EPS)
    return xc * s, s


def layout(q):
    R, D, T, RT = q.R, q.D, q.T, q.RT
    Cj = 3 * q.DT
    DMA = pltpu.SemaphoreType.DMA
    V = pltpu.VMEM
    m = SimpleNamespace()
    m.tok = V((T, R, D), BF)
    m.n1 = V((RT, D), BF)
    m.cot = V((T, R, D), BF)
    m.w = [V((D, Cj), BF), V((q.DT, D), BF), V((D, q.F), BF), V((q.F, D), BF)]
    m.qkv = V((RT, Cj), BF)
    m.prob = V((T * q.H, R, R), BF)
    m.mixed = V((RT, q.DT), BF)
    m.first = V((R, D), F32)
    m.n2 = V((T, R, D), BF)
    m.hact = V((RT, q.F), BF)
    m.dgelu = V((RT, q.F), BF)
    m.hgrad = V((RT, q.F), BF)
    m.proj = V((T, R, D), BF)
    m.fgrad = V((R, D), F32)
    m.mgrad = V((RT, q.DT), BF)
    m.jgrad = V((RT, Cj), BF)
    m.acc0 = V((R, D), F32)
    m.psend = [V((q.X, R, D), BF) for _ in range(2)]
    m.precv = [V((q.X, R, D), BF) for _ in range(2)]
    m.xsend = [V((R, D) if q.X == 2 else (16, 128), BF) for _ in range(2)]
    m.xrecv = [V((R, D) if q.X == 2 else (16, 128), BF) for _ in range(2)]
    m.rs = [[DMA((q.X,)), DMA((q.X,)), DMA((1,)), DMA((1,))] for _ in range(4)]
    m.dw = [V((bz, q.Y * rb, C), BF) for bz, rb, C in q.grads]
    m.yr = [V((q.Y - 1, bz, rb, C), BF) for bz, rb, C in q.grads]
    m.zr = [V((q.OS if w == O else q.Z - 1, rb, C), BF) for w, (bz, rb, C) in enumerate(q.grads)]
    m.zq = [V((16, 128) if w == O else (rb, C), BF) for w, (bz, rb, C) in enumerate(q.grads)]
    m.fin = [V((1 if w == O else T, rb, C), BF) for w, (bz, rb, C) in enumerate(q.grads)]
    m.sy = [[DMA((q.Y - 1, bz)), DMA((q.Y - 1, bz))] for bz, rb, C in q.grads]
    m.sz = [[DMA((max(q.Z - 1, q.ZT),)), DMA((max(q.Z, q.OS),))] for _ in q.grads]
    m.sout = [DMA((T, q.n)) for _ in q.grads]
    m.gz = [[DMA((q.Z,)), DMA((max(q.Z - 1, q.ZT),))] for _ in range(5)]
    m.gy = [[DMA((q.Y - 1, q.Z)), DMA((q.Y - 1, q.Z))] for _ in range(5)]
    m.hy = [DMA((q.Y - 1,)), DMA((q.Y - 1,))]
    m.hz = [DMA((q.Y, q.Z)), DMA((q.Y, max(q.Z - 1, 1)))]
    pair = lambda: [DMA((3,)), DMA((3,))]
    m.ttok, m.tcot, m.tn2, m.tproj, m.tcnt, m.tfo = (pair() for _ in range(6))
    m.tfin = [pair() for _ in q.grads]
    m.vec = V((q.n, VROWS, q.Dn), BF)
    m.vf = V((8, D), F32)
    m.hb = V((8, q.F), F32)
    m.cnt = V((T, 8, 128), jnp.int32)
    m.vg = V((8, D), F32)
    m.vgh = V((8, q.F), F32)
    m.v3 = V((q.n, VROWS, q.Dn), F32)
    m.v3c = V((2, q.n, VROWS, q.Dn), F32)
    m.v3y = V((q.Y - 1, q.Z, VROWS, q.Dn), F32)
    m.v3s = V((q.Z, VROWS, q.Dn), F32)
    m.v3z = V((q.Z - 1, VROWS, q.Dn), F32)
    m.vout = V((VROWS, q.Dn), F32)
    m.svt = [DMA((2,)), DMA((2,))]
    m.svy = [DMA((q.Y - 1, q.Z)), DMA((q.Y - 1, q.Z))]
    m.svz = [DMA((q.Z - 1,)), DMA((q.Z - 1,))]
    m.loc = DMA((7 + q.n,))
    return vars(m)


def kernel(q, tree, *refs):
    (tokens, counts, joint_w, out_w, exp_w, shr_w, cotangent) = refs[:7]
    vectors = refs[7:16]
    (o_out, o_tg, o_vec, o_j, o_o, o_e, o_s) = refs[16:23]
    b = SimpleNamespace(**jax.tree.unflatten(tree, refs[23:]))
    R, D, T, X, RT, n, Y, Z = q.R, q.D, q.T, q.X, q.RT, q.n, q.Y, q.Z
    Dn, DT, F, FB, H, hd, ZT = q.Dn, q.DT, q.F, q.FB, q.H, q.hd, q.ZT
    Cj = 3 * DT

    dp = lax.axis_index("dp")
    s = lax.axis_index("fsdp")
    t = dp % T
    c, xx = t % 2, t // 2
    y, z = s % Y, s // Y
    core = (dp + 1 - 2 * c, s)
    xdp = dp + 2 - 4 * xx
    xpeer = (xdp, s)
    xcore = (xdp + 1 - 2 * c, s)
    tc = t + 1 - 2 * c
    if X == 2:
        tx = t + 2 - 4 * xx
        txc = tx + 1 - 2 * c
    zid = [flip(z, k) for k in range(Z)]
    relay = Z == 4
    inner = jnp.logical_and(z > 0, z < Z - 1)
    outer = jnp.logical_not(inner)
    zfar = jnp.where(z > 1, Z - 1, 0)
    yid = [(y + k) % Y for k in range(Y)]
    ysrc = [(y + Y - k) % Y for k in range(Y)]
    zpeer = [(dp, zid[k] * Y + y) for k in range(Z)]
    ypeer = [(dp, z * Y + yid[k]) for k in range(Y)]
    pending, pending_if = [], []

    def rc(src, dst, ss, rs, dev):
        return pltpu.make_async_remote_copy(
            src_ref=src, dst_ref=dst, send_sem=ss, recv_sem=rs,
            device_id=dev, device_id_type=MESH)

    def go(cp):
        cp.start()
        pending.append(cp)
        return cp

    def go_if(pred, cp):
        pl.when(pred)(cp.start)
        pending_if.append((pred, cp))

    loc = b.loc
    cp_tok = pltpu.make_async_copy(tokens, b.tok.at[t], loc.at[0])
    cp_cot = pltpu.make_async_copy(cotangent, b.cot.at[t], loc.at[1])
    cp_shr = pltpu.make_async_copy(
        shr_w.at[ds(t * FB, FB, 16)], b.w[S].at[ds(s * FB, FB, 16)], loc.at[3])
    cp_j = [pltpu.make_async_copy(
        joint_w.at[:, ds(j * D + t * DT, DT, 128)],
        b.w[J].at[ds(s * Dn, Dn, 16), pl.ds(j * DT, DT)], loc.at[4 + j]) for j in range(3)]
    cp_e = [pltpu.make_async_copy(
        exp_w.at[:, ds(i * (T * FB) + t * FB, FB, 128)],
        b.w[E].at[ds(s * Dn, Dn, 16), pl.ds(i * FB, FB)], loc.at[7 + i]) for i in range(n)]
    for cp in cp_j + [cp_tok] + cp_e + [cp_shr, cp_cot]:
        cp.start()

    lane = lax.broadcasted_iota(jnp.int32, (8, 128), 1)
    cv = jnp.zeros((8, 128), jnp.int32)
    for i in range(q.slots):
        cv = jnp.where(lane == i, counts[0, i], cv)
    b.cnt[t] = cv

    bar = pltpu.get_barrier_semaphore()
    greet = [core] + ([xpeer, xcore] if X == 2 else []) + zpeer[1:] + ypeer[1:]
    for dev in greet:
        pl.semaphore_signal(bar, inc=1, device_id=dev, device_id_type=MESH)
    pl.semaphore_wait(bar, len(greet))

    def slot(w, src_s):
        if w == VEC:
            return b.vec.at[src_s]
        if w == S:
            return b.w[S].at[ds(src_s * FB, FB // 2, 16)]
        return b.w[w].at[ds(src_s * Dn, Dn, 16)]

    def gz_copy(w, k):
        return rc(slot(w, s), slot(w, s), b.gz[w][0].at[k - 1], b.gz[w][1].at[k - 1], zpeer[k])

    def gz_wait(w, k):
        src = slot(w, zid[k] * Y + y)
        rc(src, src, b.gz[w][0].at[k - 1], b.gz[w][1].at[k - 1], zpeer[k]).wait_recv()

    def gy_copies(w, k):
        src = slot(w, zid[k] * Y + y)
        return [rc(src, src, b.gy[w][0].at[m - 1, k], b.gy[w][1].at[m - 1, k], ypeer[m])
                for m in range(1, Y)]

    def ag_z(w):
        if not relay or w == VEC:
            for k in range(1, Z):
                go(gz_copy(w, k))
            return
        go(gz_copy(w, 1))
        go_if(inner, gz_copy(w, 3))
        go(gz_copy(w, 2))

    def ag_y(w, k):
        if k:
            gz_wait(w, k)
        if relay and w != VEC and k == 2:
            src = slot(w, zid[k] * Y + y)
            go_if(inner, rc(src, src, b.gz[w][0].at[Z - 1], b.gz[w][1].at[2], (dp, zfar * Y + y)))
        for cp in gy_copies(w, k):
            go(cp)

    def ag_y_if(pred, w, k):
        @pl.when(pred)
        def _():
            gz_wait(w, k)
            for cp in gy_copies(w, k):
                cp.start()

    def fw(w, *steps):
        for i in steps:
            if not relay or w == VEC:
                if i < Z:
                    ag_y(w, i)
            elif i == 2:
                ag_y_if(inner, w, 3)
            elif i == 4:
                ag_y_if(outer, w, 3)
                pending.extend(gy_copies(w, 3))
            else:
                ag_y(w, {0: 0, 1: 1, 3: 2}[i])

    def ag_wait(w):
        for k in range(Z):
            for m in range(1, Y):
                src = zid[k] * Y + ysrc[m]
                rc(slot(w, src), slot(w, src), b.gy[w][0].at[m - 1, k], b.gy[w][1].at[m - 1, k], ypeer[m]).wait_recv()

    def hslot(zz, yy):
        return b.w[S].at[ds((zz * Y + yy) * FB + FB // 2, FB // 2, 16)]

    def half_y(m, src):
        return rc(hslot(z, src), hslot(z, src), b.hy[0].at[m - 1], b.hy[1].at[m - 1], ypeer[m])

    def half_z(m, k, zz):
        piece = hslot(zz, ysrc[m])
        return rc(piece, piece, b.hz[0].at[m, k - 1], b.hz[1].at[m, k - 1], zpeer[k])

    def half_start():
        for m in range(1, Y):
            go(half_y(m, y))

    def half_send(*ms):
        for m in ms:
            if m:
                half_y(m, ysrc[m]).wait_recv()
            for k in ([1, 3, 2] if relay else range(1, Z)):
                if relay and k == 3:
                    go_if(inner, half_z(m, k, z))
                else:
                    go(half_z(m, k, z))

    def half_relay(m):
        if relay:
            pl.when(inner)(lambda: half_z(m, 2, zid[2]).wait_recv())
            piece = hslot(zid[2], ysrc[m])
            go_if(inner, rc(piece, piece, b.hz[0].at[m, Z - 1], b.hz[1].at[m, 2], (dp, zfar * Y + y)))

    def half_wait():
        for m in range(Y):
            for k in range(1, Z):
                if relay and k == 2:
                    pl.when(outer)(lambda m=m: half_z(m, 2, zid[2]).wait_recv())
                else:
                    half_z(m, k, zid[k]).wait_recv()

    zlo = t * ZT
    mine = z // ZT == t

    def wo_slot(zz, yy):
        return b.w[O].at[ds((zz * Y + yy) * Dn, Dn, 16)]

    def wo_z():
        @pl.when(mine)
        def _():
            zz = z - zlo
            for k in range(1, Z):
                rc(out_w, wo_slot(zz, y), b.gz[O][0].at[k - 1], b.gz[O][1].at[zz], zpeer[k]).start()
            pltpu.make_async_copy(out_w, wo_slot(zz, y), b.gz[O][1].at[zz]).start()

    def wo_y():
        for zz in range(ZT):
            pltpu.make_async_copy(out_w, wo_slot(zz, y), b.gz[O][1].at[zz]).wait()
            for m in range(1, Y):
                go(rc(wo_slot(zz, y), wo_slot(zz, y), b.gy[O][0].at[m - 1, zz], b.gy[O][1].at[m - 1, zz], ypeer[m]))

    def wo_wait():
        for zz in range(ZT):
            for m in range(1, Y):
                rc(wo_slot(zz, ysrc[m]), wo_slot(zz, ysrc[m]), b.gy[O][0].at[m - 1, zz], b.gy[O][1].at[m - 1, zz], ypeer[m]).wait_recv()

    def wo_drain():
        @pl.when(mine)
        def _():
            for k in range(1, Z):
                rc(out_w, wo_slot(z - zlo, y), b.gz[O][0].at[k - 1], b.gz[O][1].at[0], zpeer[k]).wait_send()

    def tp_send(buf, w, src=None):
        src = buf.at[t] if src is None else src
        if X == 2:
            go(rc(src, buf.at[t], w[0].at[1], w[1].at[1], xpeer))
        go(rc(src, buf.at[t], w[0].at[0], w[1].at[0], core))

    def tp_core(buf, w):
        rc(buf.at[tc], buf.at[tc], w[0].at[0], w[1].at[0], core).wait_recv()

    def tp_x(buf, w):
        if X == 2:
            rc(buf.at[tx], buf.at[tx], w[0].at[1], w[1].at[1], xpeer).wait_recv()
            go(rc(buf.at[tx], buf.at[tx], w[0].at[2], w[1].at[2], core))

    def tp_last(buf, w):
        if X == 2:
            rc(buf.at[txc], buf.at[txc], w[0].at[2], w[1].at[2], core).wait_recv()

    order = [(t, None), (tc, tp_core)] + ([(tx, tp_x), (txc, tp_last)] if X == 2 else [])

    vrow = lax.broadcasted_iota(jnp.int32, (VROWS, Dn), 0)
    packed = jnp.zeros((VROWS, Dn), F32)
    pieces = [v[...] for v in vectors[:8]]
    pieces += [vectors[8][pl.ds(r * Dn, Dn)] for r in range(vectors[8].shape[0] // Dn)]
    for i, piece in enumerate(pieces):
        packed = jnp.where(vrow == i, piece.astype(F32).reshape(1, Dn), packed)
    b.vec[s] = packed.astype(BF)
    ag_z(VEC)
    ag_y(VEC, 0)
    cnt = b.cnt
    peers = [core] + ([xpeer, xcore] if X == 2 else [])
    for i, dev in enumerate(peers):
        go(rc(cnt.at[t], cnt.at[t], b.tcnt[0].at[i], b.tcnt[1].at[i], dev))
    for cp in cp_j:
        cp.wait()
    ag_z(J)
    fw(J, 0)
    cp_tok.wait()
    tp_send(b.tok, b.ttok)
    last = range(4, max(Z, 5))

    fw(VEC, *range(1, Z))
    for cp in cp_e:
        cp.wait()
    fw(E, 0)
    ag_wait(VEC)
    vf, hb = b.vf, b.hb
    for i in range(n):
        piece = b.vec[i].astype(F32)
        vf[:, i * Dn:(i + 1) * Dn] = piece[0:8]
        kk = FB // Dn
        for r in range(kk):
            row = piece[8 + r:9 + r]
            for g in range(1, T):
                row = jnp.where(t == g, piece[8 + g * kk + r:9 + g * kk + r], row)
            hb[0:1, i * FB + r * Dn:i * FB + (r + 1) * Dn] = row
    vg, vgh = b.vg, b.vgh
    vg[...] = jnp.zeros_like(vg)

    for i, st in enumerate([tc] + ([tx, txc] if X == 2 else [])):
        rc(cnt.at[st], cnt.at[st], b.tcnt[0].at[i], b.tcnt[1].at[i], peers[i]).wait_recv()

    def ends_of(g):
        row = cnt[g]
        ends, total = [], None
        for i in range(q.slots):
            v = row[0:1, i:i + 1]
            total = v if total is None else total + v
            ends.append(total)
        return ends

    RB = 64
    nrb = R // RB

    def live_of(ends, r0, rows):
        places = lax.broadcasted_iota(jnp.int32, (rows, 1), 0) + r0
        return (places < ends[-1]).astype(F32)

    fw(J, 1)
    own_ends = ends_of(t)
    cp_cot.wait()
    cot = b.cot

    def cot_step(i, acc):
        r0 = pl.multiple_of(i * RB, RB)
        v = cot[t, pl.ds(r0, RB), :].astype(F32) * live_of(own_ends, r0, RB)
        cot[t, pl.ds(r0, RB), :] = v.astype(BF)
        return acc + jnp.sum(v, axis=0, keepdims=True)

    vg[7:8, :] = lax.fori_loop(0, nrb, cot_step, jnp.zeros((1, D), F32))
    tp_send(cot, b.tcot)

    tok, n1 = b.tok, b.n1

    def ln1(g):
        def step(i, _):
            r0 = pl.multiple_of(i * RB, RB)
            nn, _s = norm_parts(tok[g, pl.ds(r0, RB), :].astype(F32))
            n1[ds(g * R + r0, RB, RB), :] = (nn * vf[0:1, :] + vf[1:2, :]).astype(BF)
            return 0
        lax.fori_loop(0, nrb, step, 0)

    ln1(t)
    fw(J, 2)
    tp_core(tok, b.ttok)
    ln1(tc)
    wo_z()
    fw(J, 3)
    tp_x(tok, b.ttok)
    if X == 2:
        ln1(tx)
    fw(J, *last)
    if X == 2:
        tp_last(tok, b.ttok)
        ln1(txc)
    ag_wait(J)
    ag_z(E)
    qkv, wj = b.qkv, b.w[J]
    TN = 256
    for j in range(3):
        def step(i, _, j=j):
            col = j * DT + i * TN
            r = dot_nn(n1[...], wj[:, ds(col, TN, 128)])
            if j != 1:
                r = r + vf[(2 if j == 0 else 3):(3 if j == 0 else 4), ds(t * DT + i * TN, TN, 128)]
            qkv[:, ds(col, TN, 128)] = r.astype(BF)
            return 0
        lax.fori_loop(0, DT // TN, step, 0)

    wo_y()
    scale = hd ** (-0.5)
    prob, mixed = b.prob, b.mixed
    AW = 256
    GH = AW // hd
    lanes = lax.broadcasted_iota(jnp.int32, (1, AW), 1)
    head_masks = [(lanes // hd == h) for h in range(GH)]

    def hm(v, h):
        return jnp.where(head_masks[h], v, jnp.zeros_like(v))

    def attend(g):
        ends = ends_of(g)
        ri = lax.broadcasted_iota(jnp.int32, (R, R), 0)
        ci = lax.broadcasted_iota(jnp.int32, (R, R), 1)
        im_r = jnp.zeros((R, R), jnp.int32)
        im_c = jnp.zeros((R, R), jnp.int32)
        for e in ends:
            im_r = im_r + (ri >= e).astype(jnp.int32)
            im_c = im_c + (ci >= e).astype(jnp.int32)
        same = im_r == im_c
        rows = ds(g * R, R, 256)
        for a in range(DT // AW):
            qa = qkv[rows, pl.ds(a * AW, AW)]
            ka = qkv[rows, pl.ds(DT + a * AW, AW)]
            va = qkv[rows, pl.ds(2 * DT + a * AW, AW)]
            acc = None
            for h in range(GH):
                sc = dot_nt(hm(qa, h), ka) * scale
                sc = jnp.where(same, sc, MASKED)
                top = jnp.max(sc, axis=-1, keepdims=True)
                ex = jnp.exp(sc - top)
                tot = jnp.sum(ex, axis=-1, keepdims=True)
                p = (ex * (1.0 / tot)).astype(BF)
                prob[g * H + a * GH + h] = p
                part = dot_nn(p, hm(va, h))
                acc = part if acc is None else acc + part
            mixed[rows, pl.ds(a * AW, AW)] = acc.astype(BF)

    def att_step(g, _):
        attend(g)
        return 0

    lax.fori_loop(0, T, att_step, 0)
    cp_shr.wait()
    ag_z(S)
    half_send(0)
    fw(E, 1)
    wo_wait()

    acc0 = b.acc0

    def block_mm(lhs, g, rhs, nt, put):
        def step(i, _):
            cols = ds(i * TN, TN, 256)
            a = lhs[ds(g * R, R, 256), :]
            put(cols, dot_nt(a, rhs[cols, :]) if nt else dot_nn(a, rhs[:, cols]))
            return 0
        lax.fori_loop(0, D // TN, step, 0)

    def rs_copy(u, r, i):
        return rc(b.psend[u].at[i], b.precv[u].at[i], b.rs[r][0].at[i], b.rs[r][1].at[i], core)

    def rs_xcopy(u, r):
        return rc(b.xsend[u], b.xrecv[u], b.rs[r][2].at[0], b.rs[r][3].at[0], xpeer)

    def rs_start(u, r, lhs, rhs, nt, put_own=None):
        ps = b.psend[u]

        def put_at(i):
            def put(cols, v):
                ps[i, :, cols] = v.astype(BF)
            return put

        def put_acc(cols, v):
            acc0[:, cols] = v

        if X == 2:
            block_mm(lhs, txc, rhs, nt, put_at(1))
            rs_copy(u, r, 1).start()
            block_mm(lhs, tx, rhs, nt, put_acc)
            rs_copy(u, r, 1).wait_recv()
            pr, xs = b.precv[u], b.xsend[u]

            def add(i, _):
                rows = ds(i * RB, RB, RB)
                xs[rows, :] = (acc0[rows, :] + pr[1, rows, :].astype(F32)).astype(BF)
                return 0
            lax.fori_loop(0, nrb, add, 0)
            rs_xcopy(u, r).start()
        block_mm(lhs, tc, rhs, nt, put_at(0))
        rs_copy(u, r, 0).start()
        block_mm(lhs, t, rhs, nt, put_own or put_acc)

    def rs_wait(u, r):
        rs_copy(u, r, 0).wait_recv()
        if X == 2:
            rs_xcopy(u, r).wait_recv()

    def rs_value(u, rows, own=True):
        v = b.precv[u][0, rows, :].astype(F32)
        if own:
            v = acc0[rows, :] + v
        if X == 2:
            v = v + b.xrecv[u][rows, :].astype(F32)
        return v

    def rs_done(u, r):
        for i in range(X):
            rs_copy(u, r, i).wait_send()
        if X == 2:
            rs_xcopy(u, r).wait_send()

    rs_start(0, 0, mixed, b.w[O], False)
    tp_core(cot, b.tcot)
    tp_x(cot, b.tcot)
    fw(E, 2)
    fw(E, 3)
    half_start()
    fw(S, 0)
    fw(E, *last)
    rs_wait(0, 0)
    first, n2 = b.first, b.n2

    def ln2(i, _):
        rows = ds(i * RB, RB, RB)
        v = tok[t, rows, :].astype(F32) + (rs_value(0, rows) + vf[4:5, :])
        first[rows, :] = v
        nn, _s = norm_parts(v)
        n2[t, rows, :] = (nn * vf[5:6, :] + vf[6:7, :]).astype(BF)
        return 0
    lax.fori_loop(0, nrb, ln2, 0)
    tp_send(n2, b.tn2)
    rs_done(0, 0)
    tp_last(cot, b.tcot)
    half_send(*range(1, Y))
    fw(S, 1)
    ag_wait(E)

    hact, dgelu, we, ws = b.hact, b.dgelu, b.w[E], b.w[S]

    def up(g):
        def step(i, _):
            cols = ds(i * TN, TN, 256)
            rows = ds(g * R, R, 256)
            h = dot_nn(n2[g], we[:, cols]) + hb[0:1, cols]
            phi = 0.5 * (1.0 + lax.erf(h * 0.7071067811865476))
            hact[rows, cols] = (h * phi).astype(BF)
            dgelu[rows, cols] = (phi + h * (jnp.exp(-0.5 * h * h) * 0.3989422804014327)).astype(BF)
            return 0
        lax.fori_loop(0, F // TN, step, 0)

    up(t)
    tp_core(n2, b.tn2)
    up(tc)
    fw(S, 2)
    fw(S, 3)
    half_relay(0)
    tp_x(n2, b.tn2)
    if X == 2:
        up(tx)
        tp_last(n2, b.tn2)
        up(txc)
    fw(S, *last)

    def blocks(w):
        return q.grads[w]

    def dw_dest(w, k):
        return zlo + k if w == O else zid[k]

    def dw_slot(w, k):
        return k if w == O else zid[k]

    def dw_y(w, sl, m):
        rb = blocks(w)[1]
        return rc(b.dw[w].at[sl, ds(yid[m] * rb, rb, 16)], b.yr[w].at[m - 1, sl],
                  b.sy[w][0].at[m - 1, sl], b.sy[w][1].at[m - 1, sl], ypeer[m])

    def dw_compute(w, k, lhs, rhs):
        bz, rb, C = blocks(w)
        sl = dw_slot(w, k)
        tile = Y * rb
        TC = next(v for v in (512, 768, 256) if C % v == 0)

        def step(i, _):
            cols = ds(i * TC, TC, 256)
            for r in range(tile // 256):
                a = lhs(sl * tile + r * 256)
                b.dw[w][sl, pl.ds(r * 256, 256), cols] = dot_tn(a, rhs(cols)).astype(BF)
            return 0
        lax.fori_loop(0, C // TC, step, 0)
        for m in range(1, Y):
            go(dw_y(w, sl, m))

    def dw_sum(w, k):
        bz, rb, C = blocks(w)
        sl = dw_slot(w, k)
        for m in range(1, Y):
            dw_y(w, sl, m).wait_recv()
        ch = 64

        def add(i, _):
            rows = ds(y * rb + i * ch, ch, 64)
            v = b.dw[w][sl, rows, :].astype(F32)
            for m in range(1, Y):
                v = v + b.yr[w][m - 1, sl, ds(i * ch, ch, 64), :].astype(F32)
            b.dw[w][sl, rows, :] = v.astype(BF)
            return 0
        lax.fori_loop(0, rb // ch, add, 0)

    def dw_z(w, k):
        rb = blocks(w)[1]
        return rc(b.dw[w].at[zid[k], ds(y * rb, rb, 16)], b.zr[w].at[k - 1],
                  b.sz[w][0].at[k - 1], b.sz[w][1].at[k - 1], zpeer[k])

    def dw_o(zz, i, to):
        return rc(b.dw[O].at[zz, ds(y * Dn, Dn, 16)], b.zr[O].at[i], b.sz[O][0].at[zz],
                  b.sz[O][1].at[i], (dp, to * Y + y))

    def relay_slot(zz):
        return zz if ZT <= 2 else 2 + zz

    def dw_relay(w):
        rb = blocks(w)[1]
        return rc(b.dw[w].at[zid[3], ds(y * rb, rb, 16)], b.zq[w], b.sz[w][0].at[2],
                  b.sz[w][1].at[Z - 1], zpeer[1])

    def dw_send(w, k):
        dw_sum(w, k)
        if relay and k == 3:
            go_if(inner, dw_z(w, k))
            go_if(outer, dw_relay(w))
            return
        if relay and k == 2:
            @pl.when(inner)
            def _():
                dw_relay(w).wait_recv()
                rb, ch = blocks(w)[1], 64

                def add(i, _):
                    rows = ds(y * rb + i * ch, ch, 64)
                    v = b.dw[w][zid[2], rows, :].astype(F32) + b.zq[w][ds(i * ch, ch, 64), :].astype(F32)
                    b.dw[w][zid[2], rows, :] = v.astype(BF)
                    return 0
                lax.fori_loop(0, rb // ch, add, 0)
        if k:
            go(dw_z(w, k))

    def dwo_hops(act_near, act_far):
        for zz in range(ZT):
            zo = zlo + zz
            far = z // 2 != zo // 2
            near = jnp.logical_and(z // 2 == zo // 2, z != zo)
            if Z > 1:
                pl.when(near)(lambda zz=zz, zo=zo: act_near(dw_o(zz, 0, zo)))
            if Z > 2:
                pl.when(jnp.logical_and(far, outer))(lambda zz=zz: act_near(dw_o(zz, relay_slot(zz), zid[1])))
                pl.when(jnp.logical_and(far, inner))(lambda zz=zz, zo=zo: act_far(zz, dw_o(zz, 1, zo)))

    def dwo_first():
        for zz in range(ZT):
            dw_sum(O, zz)
        dwo_hops(lambda cp: cp.start(), lambda zz, cp: None)

    def dwo_second():
        def pass_on(zz, cp):
            dw_o(zz, relay_slot(zz), z).wait_recv()
            ch = 64

            def add(j, _):
                rows = ds(y * Dn + j * ch, ch, 64)
                v = b.dw[O][zz, rows, :].astype(F32) + b.zr[O][relay_slot(zz), ds(j * ch, ch, 64), :].astype(F32)
                b.dw[O][zz, rows, :] = v.astype(BF)
                return 0
            lax.fori_loop(0, Dn // ch, add, 0)
            cp.start()
        dwo_hops(lambda cp: None, pass_on)

    def dw_final(w):
        bz, rb, C = blocks(w)
        ch = 64
        fin = b.fin[w]
        own = z - zlo if w == O else z
        me = 0 if w == O else t

        def total(slots):
            def add(i, _):
                rows = ds(i * ch, ch, 64)
                v = b.dw[w][own, ds(y * rb + i * ch, ch, 64), :].astype(F32)
                for i_slot in slots:
                    v = v + b.zr[w][i_slot, rows, :].astype(F32)
                fin[me, rows, :] = v.astype(BF)
                return 0
            lax.fori_loop(0, rb // ch, add, 0)

        def wait_total(ks):
            for k in ks:
                dw_z(w, k).wait_recv()
            total([k - 1 for k in ks])

        if w == O:
            ends = range(min(Z - 1, 2))
            for i in ends:
                dw_o(own, i, z).wait_recv()
            total(ends)
        elif relay:
            pl.when(inner)(lambda: wait_total((1, 2, 3)))
            pl.when(outer)(lambda: wait_total((1, 2)))
        else:
            wait_total(range(1, Z))
        if w != O:
            tp_send(fin, b.tfin[w])

    def out_copies(w, g):
        fin, so = b.fin[w], b.sout[w]
        if w == J:
            return [pltpu.make_async_copy(fin.at[g, :, pl.ds(j * DT, DT)],
                    o_j.at[:, ds(j * D + g * DT, DT, 128)], so.at[g, j]) for j in range(3)]
        if w == E:
            return [pltpu.make_async_copy(fin.at[g, :, pl.ds(i * FB, FB)],
                    o_e.at[:, ds(i * (T * FB) + g * FB, FB, 128)], so.at[g, i]) for i in range(n)]
        return [pltpu.make_async_copy(fin.at[g], o_s.at[ds(g * FB, FB, 16)], so.at[g, 0])]

    def cot_rhs(cols):
        return cot[:, :, cols].reshape(RT, cols.size)

    zorder = ([3, 2, 1] if relay else list(range(1, Z))) + [0]
    half = len(zorder) // 2

    def dw_shrink(ks):
        for k in ks:
            dw_compute(S, k, lambda c0: hact[:, ds(c0, 256, 256)], cot_rhs)

    dw_shrink(zorder[:half])
    for m in range(1, Y):
        half_relay(m)
    dw_shrink(zorder[half:])
    ag_wait(S)
    half_wait()
    hgrad = b.hgrad

    def down(i, _):
        cols = ds(i * TN, TN, 256)
        v = dot_nt(cot[...].reshape(RT, D), ws[cols, :]) * dgelu[:, cols].astype(F32)
        hgrad[:, cols] = v.astype(BF)
        return 0

    lax.fori_loop(0, F // TN, down, 0)
    def send(w, *steps):
        for i in steps:
            if i < Z:
                dw_send(w, zorder[i])

    rs_start(0, 1, hgrad, we, True)
    send(S, 0)

    def dw_expand(ks):
        for k in ks:
            dw_compute(E, k, lambda c0: n2[:, :, ds(c0, 256, 256)].reshape(RT, 256),
                       lambda cols: hgrad[:, cols])

    dw_expand(zorder[:half])
    send(S, 1)
    dw_expand(zorder[half:])
    send(S, 2)
    rs_wait(0, 1)
    proj, fgrad = b.proj, b.fgrad

    def ln2_back(i, carry):
        ag_, as_, ab_ = carry
        rows = ds(i * RB, RB, RB)
        two = rs_value(0, rows)
        nn, sd = norm_parts(first[rows, :])
        e = two * vf[5:6, :]
        og = cot[t, rows, :].astype(F32)
        fg = og + sd * (e - jnp.mean(e, axis=-1, keepdims=True)
                        - nn * jnp.mean(e * nn, axis=-1, keepdims=True))
        fgrad[rows, :] = fg
        pj = fg.astype(BF)
        proj[t, rows, :] = pj
        return (ag_ + jnp.sum(two * nn, axis=0, keepdims=True),
                as_ + jnp.sum(two, axis=0, keepdims=True),
                ab_ + jnp.sum(pj.astype(F32), axis=0, keepdims=True))

    zrow = jnp.zeros((1, D), F32)
    g2, s2, ob = lax.fori_loop(0, nrb, ln2_back, (zrow, zrow, zrow))
    tp_send(proj, b.tproj)
    vg[5:6, :] = g2
    vg[6:7, :] = s2
    vg[4:5, :] = ob
    rs_done(0, 1)

    send(S, *range(3, Z))
    def add_to_first(cols, v):
        first[:, cols] = first[:, cols] + v

    rs_start(1, 2, hact, ws, False, add_to_first)

    def hb_step(i, _):
        cols = ds(i * TN, TN, 256)
        vgh[0:1, cols] = jnp.sum(hgrad[:, cols].astype(F32), axis=0, keepdims=True)
        return 0
    lax.fori_loop(0, F // TN, hb_step, 0)
    mgrad, jgrad, wo = b.mgrad, b.jgrad, b.w[O]

    def mixed_back(g):
        def step(i, _):
            cols = ds(i * TN, TN, 256)
            mgrad[ds(g * R, R, 256), cols] = dot_nt(proj[g], wo[cols, :]).astype(BF)
            return 0
        lax.fori_loop(0, DT // TN, step, 0)

    def attend_back(g):
        rows = ds(g * R, R, 256)
        for a in range(DT // AW):
            qa = qkv[rows, pl.ds(a * AW, AW)]
            ka = qkv[rows, pl.ds(DT + a * AW, AW)]
            va = qkv[rows, pl.ds(2 * DT + a * AW, AW)]
            ma = mgrad[rows, pl.ds(a * AW, AW)]
            aq = ak = av = None
            for h in range(GH):
                mh = hm(ma, h)
                pg = dot_nt(mh, va)
                pl_ = prob[g * H + a * GH + h]
                p = pl_.astype(F32)
                inner = jnp.sum(p * pg, axis=-1, keepdims=True)
                sg = (p * (pg - inner)).astype(BF)
                dq = dot_nn(sg, hm(ka, h))
                dk = dot_tn(sg, hm(qa, h))
                dv = dot_tn(pl_, mh)
                aq = dq if aq is None else aq + dq
                ak = dk if ak is None else ak + dk
                av = dv if av is None else av + dv
            jgrad[rows, pl.ds(a * AW, AW)] = (aq * scale).astype(BF)
            jgrad[rows, pl.ds(DT + a * AW, AW)] = (ak * scale).astype(BF)
            jgrad[rows, pl.ds(2 * DT + a * AW, AW)] = av.astype(BF)

    obuf = n2.at[tc]

    def out_step(i, _):
        rows = ds(i * RB, RB, RB)
        r0 = i * RB
        v = (first[rows, :] + rs_value(1, rows, False) + vf[7:8, :]) * live_of(own_ends, r0, RB)
        obuf[rows, :] = v.astype(BF)
        return 0
    def attb_step(g, _):
        attend_back(g)
        return 0

    send(E, 0)
    mixed_back(t)
    tp_core(proj, b.tproj)
    mixed_back(tc)
    attend_back(t)
    tp_x(proj, b.tproj)
    attend_back(tc)
    if X == 2:
        mixed_back(tx)
        attend_back(tx)
    send(E, 1)
    tp_last(proj, b.tproj)
    dw_final(S)
    for zz in range(ZT):
        dw_compute(O, zz, lambda c0: mixed[:, ds(c0, 256, 256)],
                   lambda cols: proj[:, :, cols].reshape(RT, cols.size))
    if X == 2:
        mixed_back(txc)
        attend_back(txc)
    send(E, 2)
    rs_start(0, 3, jgrad, wj, True)
    for k in zorder:
        dw_compute(J, k, lambda c0: n1[:, ds(c0, 256, 256)], lambda cols: jgrad[:, cols])
    dwo_first()
    send(E, *range(3, Z))
    dw_final(E)
    rs_wait(1, 2)
    lax.fori_loop(0, nrb, out_step, 0)
    cp_out = pltpu.make_async_copy(obuf, o_out, loc.at[0])
    cp_out.start()
    for i in range(2):
        j = 2 * i
        vg[2 + i:3 + i, ds(t * DT, DT, 128)] = jnp.sum(
            jgrad[:, pl.ds(j * DT, DT)].astype(F32), axis=0, keepdims=True)
    send(J, 0)
    dwo_second()
    send(J, 1)
    send(J, 2)
    rs_wait(0, 3)
    tbuf = proj.at[tc]

    def ln1_back(i, carry):
        ag_, as_ = carry
        rows = ds(i * RB, RB, RB)
        one = rs_value(0, rows)
        nn, sd = norm_parts(tok[t, rows, :].astype(F32))
        e = one * vf[0:1, :]
        v = fgrad[rows, :] + sd * (e - jnp.mean(e, axis=-1, keepdims=True)
                                   - nn * jnp.mean(e * nn, axis=-1, keepdims=True))
        tbuf[rows, :] = v.astype(BF)
        return (ag_ + jnp.sum(one * nn, axis=0, keepdims=True),
                as_ + jnp.sum(one, axis=0, keepdims=True))

    g1, s1 = lax.fori_loop(0, nrb, ln1_back, (zrow, zrow))
    cp_tg = pltpu.make_async_copy(tbuf, o_tg, loc.at[1])
    cp_tg.start()
    vg[0:1, :] = g1
    vg[1:2, :] = s1

    v3, v3c = b.v3, b.v3c
    kk = FB // Dn
    v3[...] = jnp.zeros_like(v3)
    for i in range(n):
        v3[i, 0:8, :] = vg[:, i * Dn:(i + 1) * Dn]
        for r in range(kk):
            row = vgh[0:1, i * FB + r * Dn:i * FB + (r + 1) * Dn]
            for g in range(T):
                v3[i, 8 + g * kk + r:9 + g * kk + r, :] = jnp.where(t == g, row, jnp.zeros_like(row))
    vt = rc(v3, v3c.at[0], b.svt[0].at[0], b.svt[1].at[0], core)
    vt.start()
    send(J, *range(3, Z))
    vt.wait()
    v3[...] = v3[...] + v3c[0]
    if X == 2:
        vx = rc(v3, v3c.at[1], b.svt[0].at[1], b.svt[1].at[1], xpeer)
        vx.start()
    owner = z // ZT

    def fo_copy(i, dev):
        return rc(b.fin[O].at[0], b.fin[O].at[0], b.tfo[0].at[i], b.tfo[1].at[0], dev)

    @pl.when(mine)
    def _():
        dw_final(O)
        fo_copy(0, core).start()
        if X == 2:
            fo_copy(1, xpeer).start()
    if X == 2:
        vx.wait()
        v3[...] = v3[...] + v3c[1]
    v3y, v3s, v3z = b.v3y, b.v3s, b.v3z

    def vy(m, k):
        return rc(v3.at[zid[k] * Y + yid[m]], v3y.at[m - 1, zid[k]], b.svy[0].at[m - 1, zid[k]],
                  b.svy[1].at[m - 1, zid[k]], ypeer[m])
    for k in range(Z):
        for m in range(1, Y):
            go(vy(m, k))

    copies = []

    def emit(w, g):
        for cp in out_copies(w, g):
            cp.start()
            copies.append(cp)

    emit(S, t)
    tp_core(b.fin[S], b.tfin[S])
    emit(S, tc)
    tp_x(b.fin[S], b.tfin[S])
    if X == 2:
        emit(S, tx)
    dw_final(J)

    def vz(k):
        return rc(v3s.at[k], v3z.at[k - 1], b.svz[0].at[k - 1], b.svz[1].at[k - 1], zpeer[k])
    for k in zorder:
        v = v3[zid[k] * Y + y]
        for m in range(1, Y):
            vy(m, k).wait_recv()
            v = v + v3y[m - 1, zid[k]]
        v3s[k] = v
        if k:
            go(vz(k))

    @pl.when(jnp.logical_not(mine))
    def _():
        fo_copy(0, core).wait_recv()
    if X == 2:
        pl.when(tx == owner)(lambda: fo_copy(2, core).start())
    cp_o = pltpu.make_async_copy(b.fin[O].at[0], o_o, loc.at[3])
    cp_o.start()
    emit(E, t)
    tp_core(b.fin[E], b.tfin[E])
    emit(E, tc)
    tp_x(b.fin[E], b.tfin[E])
    if X == 2:
        emit(E, tx)

    v = v3s[0]
    for k in range(1, Z):
        vz(k).wait_recv()
        v = v + v3z[k - 1]
    b.vout[...] = v
    cp_v = pltpu.make_async_copy(b.vout, o_vec, loc.at[2])
    cp_v.start()

    emit(J, t)
    tp_core(b.fin[J], b.tfin[J])
    emit(J, tc)
    tp_x(b.fin[J], b.tfin[J])
    for w in (S, E, J):
        tp_last(b.fin[w], b.tfin[w])
        if X == 2:
            emit(w, txc)
    if X == 2:
        emit(J, tx)

    for cp in pending:
        cp.wait_send()
    for pred, cp in pending_if:
        pl.when(pred)(cp.wait_send)
    for u, r in ((1, 2), (0, 3)):
        rs_done(u, r)
    wo_drain()
    dwo_hops(lambda cp: cp.wait_send(), lambda zz, cp: cp.wait_send())

    @pl.when(mine)
    def _():
        fo_copy(0, core).wait_send()
        if X == 2:
            fo_copy(1, xpeer).wait_send()
    if X == 2:
        pl.when(tx == owner)(lambda: fo_copy(2, core).wait_send())
    for cp in copies + [cp_out, cp_tg, cp_v, cp_o]:
        cp.wait()


def finish(divisor, q, *refs):
    ins, outs = refs[:7], refs[7:]
    for i in range(2):
        outs[i][...] = ins[i][...]
    for i in range(2, 6):
        outs[i][...] = ins[i][...].astype(F32) * (1.0 / divisor)

    @pl.when(pl.program_id(0) == 0)
    def _():
        v = ins[6][...] * (1.0 / divisor)
        for i in range(8):
            outs[6 + i][...] = v[i]
        for r in range(q.FF // q.D):
            outs[14][pl.ds(r * q.Dn, q.Dn)] = v[8 + r]


def body(n_dp, n_fsdp, tokens, patch_counts, gain_one, shift_one, joint_w, query_b, value_b, out_w,
         out_b, gain_two, shift_two, expand_w, expand_b, shrink_w, shrink_b, cotangent):
    R, D = tokens.shape
    q = Sizes(n_dp, n_fsdp, R, D, expand_w.shape[1], patch_counts.shape[1])
    q.grads = [(q.Z, q.Dn, 3 * q.DT), (q.ZT, q.Dn, D), (q.Z, q.Dn, q.F), (q.Z, q.FB, D)]
    scratch, tree = jax.tree.flatten(layout(q))
    anyspec = pl.BlockSpec(memory_space=pl.ANY)
    vmem = pl.BlockSpec(memory_space=pltpu.VMEM)
    sds = jax.ShapeDtypeStruct
    outs = pl.pallas_call(
        functools.partial(kernel, q, tree),
        out_shape=(
            sds((R, D), BF), sds((R, D), BF), sds((VROWS, q.Dn), F32),
            sds((q.Dn, 3 * D), BF), sds((q.Dn, D), BF), sds((q.Dn, q.FF), BF),
            sds((q.FF // q.n, D), BF)),
        in_specs=[anyspec, pl.BlockSpec(memory_space=pltpu.SMEM)] + [anyspec] * 5 + [vmem] * 9,
        out_specs=tuple([anyspec] * 7),
        scratch_shapes=scratch,
        compiler_params=pltpu.CompilerParams(
            collective_id=0, has_side_effects=True, vmem_limit_bytes=67043328),
        name="layer",
    )(tokens, patch_counts, joint_w, out_w, expand_w, shrink_w, cotangent,
      gain_one, shift_one, query_b, value_b, out_b, gain_two, shift_two, shrink_b, expand_b)
    result, tokens_grad, vec, gj, go_, ge, gs = outs
    divisor = float(n_dp * n_fsdp)
    mats = [gj, go_, ge, gs]
    if n_dp > q.T:
        groups = [[i + q.T * g for g in range(n_dp // q.T)] for i in range(q.T)]
        summed = lax.psum(tuple([vec] + mats), "dp", axis_index_groups=groups)
        vec, mats = summed[0], list(summed[1:])
    steps = 4
    blocked = lambda v: pl.BlockSpec((v.shape[0] // steps, v.shape[1]), lambda i: (i, 0))
    rows_in = [result, tokens_grad] + mats
    small = [q.Dn] * 8 + [q.FF // q.n]
    done = pl.pallas_call(
        functools.partial(finish, divisor, q),
        grid=(steps,),
        out_shape=tuple([sds(v.shape, BF) for v in rows_in[:2]] + [sds(v.shape, F32) for v in mats]
                        + [sds((k,), F32) for k in small]),
        in_specs=[blocked(v) for v in rows_in] + [vmem],
        out_specs=tuple([blocked(v) for v in rows_in] + [vmem] * 9),
        name="finish",
    )(*rows_in, vec)
    result, tokens_grad, gj, go_, ge, gs = done[:6]
    vec = done[6:]
    return (result, tokens_grad, vec[0], vec[1], gj, vec[2], vec[3], go_, vec[4], vec[5], vec[6],
            ge, vec[8], gs, vec[7])


def solution(mesh):
    rows = P(("dp", "fsdp"), None)
    vec, mat = P("fsdp"), P("fsdp", None)
    in_specs = (rows, rows, vec, vec, mat, vec, vec, mat, vec, vec, vec, mat, vec, mat, vec, rows)
    out_specs = (rows, rows, vec, vec, mat, vec, vec, mat, vec, vec, vec, mat, vec, mat, vec)
    fn = functools.partial(body, mesh.shape["dp"], mesh.shape["fsdp"])
    return jax.shard_map(fn, mesh=mesh, in_specs=in_specs, out_specs=out_specs, check_vma=False)
```
